32 devices in a mesh: rows: 16 (over z, y, core), cols: 2 (over x).
Axes of the slice: x: 2, y: 2, z: 4, core: 2. Of those that a mesh axis runs over, the one named last changes fastest.
Arguments:
- phi_start: float32 [256, 192, 384], P('rows', 'cols'), may hold values from -12 to 12
- source: float32 [256, 192, 384], P('rows', 'cols'), may hold values from -18 to 18
- owner_voxel: int32 [24576], P(('rows', 'cols')), may hold values from 0 to 589823, as said below
- column_slot: int32 [24576], replicated, may hold values from 0 to 24575, each once
- layer_matrix: float32 [1536, 24576], P('rows', 'cols'), may hold values from -0.0390625 to 0.0390625
Outputs:
- potential: float32 [256, 192, 384], P('rows', 'cols')
- boundary_phi: float32 [1536], P(('rows', 'cols'))
The draws below stay inside these ranges and needn't reach their ends.
Inputs may be any that keep to these rules, and one draw needn't show every extreme that they name: `owner_voxel`: offsets index the 16 x 96 x 384 block of the device that owns the slot, in row-major order.
All inputs are finite; a program needn't handle non-finite values.
Results may differ from the reference program's by a relative error of at most 0.00011.
Values sent between devices are 32-bit elements; how exact they have to be, the bound alone decides.
No kernel may reach another device: no remote copies, remote signals or barrier semaphores. Data moves between devices by JAX's collectives and lax.ppermute only.
A program may use at most 128 MiB of HBM per device.

```python
import jax
import jax.numpy as jnp
from jax import lax

CZ = 16
CY = 96
NX = 384
ITERS = 4
K_DEV = 768
NZ = 256
NY = 192
NB = 24576
WIN = 1536
N_ROWS = 16
N_COLS = 2


def draw_owner_voxel(key, part):
    offsets = jax.random.randint(jax.random.fold_in(key, 5), (NB,), 0, CZ * CY * NX, dtype=jnp.int32)
    offsets = offsets.at[0].set(0).at[NB - 1].set(CZ * CY * NX - 1)
    return offsets.astype(jnp.int32)


def level_of(rng, dims, cuts, least, largest):
    level, own = 1.0, jax.random.fold_in(rng, 6)
    for dim, shards_of in cuts:
        draws = jnp.exp(jax.random.uniform(jax.random.fold_in(own, dim), (shards_of,), jnp.float32, least / len(cuts), largest / len(cuts)))
        level = level * jnp.repeat(draws, dims[dim] // shards_of).reshape([-1 if axis == dim else 1 for axis in range(len(dims))])
    return level


def scatter_about(key, dims, scale, reach, pieces=(), kind=jnp.bfloat16):
    values = scale * jax.random.normal(key, dims, jnp.float32)
    if pieces:
        values = values * level_of(key, dims, pieces, -0.22, 0.18)
    return jnp.clip(values, -reach, reach).astype(kind)


def setup_inputs(seed: int = 0) -> dict:
    splits = jax.random.split(jax.random.key(seed), 6)
    phi_start = scatter_about(splits[0], (NZ, NY, NX), 2.0, 12.0, ((0, 16), (1, 2)), jnp.float32)
    source = scatter_about(splits[1], (NZ, NY, NX), 3.0, 18.0, ((0, 16), (1, 2)), jnp.float32)
    owner_voxel = draw_owner_voxel(jax.random.fold_in(splits[5], 71), 0)
    column_slot = jax.random.permutation(splits[3], NB).astype(jnp.int32)
    layer_matrix = scatter_about(splits[4], (WIN, NB), NB ** -0.5, 0.0390625, ((0, 16), (1, 2)), jnp.float32)
    return {"phi_start": phi_start, "source": source, "owner_voxel": owner_voxel, "column_slot": column_slot, "layer_matrix": layer_matrix}


def relax(potential, source):
    padded = jnp.pad(potential, 1)
    neighbours = padded[2:, 1:-1, 1:-1] + padded[:-2, 1:-1, 1:-1]
    neighbours = neighbours + padded[1:-1, 2:, 1:-1] + padded[1:-1, :-2, 1:-1]
    neighbours = neighbours + padded[1:-1, 1:-1, 2:] + padded[1:-1, 1:-1, :-2]
    return (source + neighbours) / 6.0


def reference(phi_start, source, owner_voxel, column_slot, layer_matrix):
    potential = phi_start
    for sweep_index in range(ITERS):
        potential = relax(potential, source)
    blocks = potential.reshape(N_ROWS, CZ, N_COLS, CY, NX).transpose(0, 2, 1, 3, 4).reshape(-1)
    slot_owner = (jnp.arange(NB, dtype=jnp.int32) // K_DEV).astype(jnp.int32)
    flat_index = (slot_owner * (CZ * CY * NX) + owner_voxel).astype(jnp.int32)
    node_values = blocks[flat_index]
    trace = node_values[column_slot]
    boundary_phi = jnp.dot(layer_matrix, trace, precision=lax.Precision.HIGHEST, preferred_element_type=jnp.float32)
    return potential, boundary_phi
```

```python
import jax
import jax.numpy as jnp
from jax import lax
from jax.experimental import pallas as pl
from jax.experimental.pallas import tpu as pltpu
from jax.sharding import PartitionSpec as P

LANES = 128
BOTH = ("rows", "cols")


def window_kernel(col_ref, table_ref, slot_ref, matrix_hbm, keep_ref, send_ref, matrix_ref, trace_ref, rows_ref, sem):
    copy = pltpu.make_async_copy(matrix_hbm, matrix_ref, sem)
    copy.start()
    owners, width = table_ref.shape
    parts = width // LANES
    chunks = trace_ref.shape[0]
    for q in range(parts):
        rows_ref[q * owners:(q + 1) * owners, :] = table_ref[:, q * LANES:(q + 1) * LANES]
    half = chunks
    group = 12
    first = col_ref[0] * half

    def gather_group(g, carry):
        base = pl.multiple_of(g * (group * 8), 8)
        slots = [slot_ref[pl.ds(pl.multiple_of(first + base + 8 * v, 8), 8), :] for v in range(group)]
        low = [s & (LANES - 1) for s in slots]
        high = [s >> 7 for s in slots]

        def owner_step(d, accs):
            accs = list(accs)
            for q in range(parts):
                row = jnp.broadcast_to(rows_ref[pl.ds(q * owners + d, 1), :], (8, LANES))
                number = d * parts + q
                for v in range(group):
                    picked = jnp.take_along_axis(row, low[v], axis=1)
                    accs[v] = jnp.where(high[v] == number, picked, accs[v])
            return tuple(accs)

        zero = jnp.zeros((8, LANES), jnp.float32)
        accs = lax.fori_loop(0, owners, owner_step, (zero,) * group)
        for v in range(group):
            trace_ref[pl.ds(pl.multiple_of(base + 8 * v, 8), 8), :] = accs[v]
        return carry

    lax.fori_loop(0, chunks // (8 * group), gather_group, 0)
    copy.wait()
    rows = matrix_ref.shape[0]
    blocks = rows // 16
    start = [pl.multiple_of(col_ref[0] * (rows // 2), 8), pl.multiple_of((1 - col_ref[0]) * (rows // 2), 8)]

    def chunk_step(c, accs):
        accs = list(accs)
        for u in range(8):
            at = pl.multiple_of((c * 8 + u) * LANES, LANES)
            value = jnp.broadcast_to(trace_ref[pl.ds(c * 8 + u, 1), :], (8, LANES))
            for side in range(2):
                for b in range(blocks):
                    tile = matrix_ref[pl.ds(start[side] + 8 * b, 8), pl.ds(at, LANES)]
                    accs[side * blocks + b] = accs[side * blocks + b] + tile * value
        return tuple(accs)

    zero = jnp.zeros((8, LANES), jnp.float32)
    accs = lax.fori_loop(0, chunks // 8, chunk_step, (zero,) * (2 * blocks))
    for side, out in enumerate((keep_ref, send_ref)):
        stack = jnp.concatenate(accs[side * blocks:(side + 1) * blocks] + (zero,) * (16 - blocks), axis=0)
        out[...] = jnp.sum(stack.T, axis=0, keepdims=True)


def window_product(col, table, slots, matrix):
    rows, columns = matrix.shape
    chunks = columns // LANES
    out = jax.ShapeDtypeStruct((1, LANES), jnp.float32)
    vmem = pl.BlockSpec(memory_space=pltpu.VMEM)
    return pl.pallas_call(
        window_kernel,
        out_shape=(out, out),
        in_specs=[pl.BlockSpec(memory_space=pltpu.SMEM), vmem, vmem, pl.BlockSpec(memory_space=pl.ANY)],
        out_specs=(vmem, vmem),
        scratch_shapes=[
            pltpu.VMEM((rows, columns), jnp.float32),
            pltpu.VMEM((chunks, LANES), jnp.float32),
            pltpu.VMEM((table.size // LANES, LANES), jnp.float32),
            pltpu.SemaphoreType.DMA,
        ],
        compiler_params=pltpu.CompilerParams(vmem_limit_bytes=48 << 20),
    )(col, table, slots, matrix)


def with_halo(value, sides, width):
    for axis, dim in sides:
        size, length = (lax.axis_size(axis), value.shape[dim])
        up = [(i, (i + 1) % size) for i in range(size - 1)]
        down = [(j, i) for i, j in up]
        last = lax.slice_in_dim(value, length - width, length, axis=dim)
        first = lax.slice_in_dim(value, 0, width, axis=dim)
        before = lax.ppermute(last, axis, up)
        after = lax.ppermute(first, axis, down)
        value = jnp.concatenate([before, value, after], axis=dim)
    return value


def neighbour_sum(padded):
    padded = jnp.pad(padded, ((0, 0), (0, 0), (1, 1)))
    neighbours = padded[2:, 1:-1, 1:-1] + padded[:-2, 1:-1, 1:-1]
    neighbours = neighbours + padded[1:-1, 2:, 1:-1] + padded[1:-1, :-2, 1:-1]
    neighbours = neighbours + padded[1:-1, 1:-1, 2:] + padded[1:-1, 1:-1, :-2]
    return neighbours


ITERS = 4


def local(phi_start, source, owner_voxel, column_slot, layer_matrix):
    potential = phi_start
    for sweep_index in range(ITERS):
        padded = with_halo(potential, (("rows", 0), ("cols", 1)), 1)
        potential = (source + neighbour_sum(padded)) / 6.0
    node_values = potential.reshape(-1)[owner_voxel]
    col = lax.axis_index("cols")
    devices = lax.axis_size(BOTH)
    table = lax.all_to_all(jnp.broadcast_to(node_values[None], (devices, node_values.shape[0])), BOTH, 0, 0)
    slots = column_slot.reshape(-1, LANES)
    keep, send = window_product(col.astype(jnp.int32)[None], table, slots, layer_matrix)
    received = lax.ppermute(send, "cols", [(0, 1), (1, 0)])
    half = layer_matrix.shape[0] // 2
    return potential, (keep + received)[0, :half]


def solution(mesh):
    return jax.shard_map(
        local,
        mesh=mesh,
        in_specs=(
            P("rows", "cols", None),
            P("rows", "cols", None),
            P(("rows", "cols")),
            P(),
            P("rows", "cols"),
        ),
        out_specs=(P("rows", "cols", None), P(("rows", "cols"))),
        check_vma=False,
    )
```

```python
import functools

import jax
import jax.numpy as jnp
from jax import lax
from jax.experimental import pallas as pl
from jax.experimental.pallas import tpu as pltpu
from jax.sharding import PartitionSpec as P

ITERS = 4
LANES = 128
SUB = 8
SIXTH = 1.0 / 6.0
BOTH = ("rows", "cols")
VMEM = pl.BlockSpec(memory_space=pltpu.VMEM)
SMEM = pl.BlockSpec(memory_space=pltpu.SMEM)
ANY = pl.BlockSpec(memory_space=pl.ANY)


def lanes_of(shape=(SUB, LANES)):
    return lax.broadcasted_iota(jnp.int32, shape, 1)


def subs_of(shape=(SUB, LANES)):
    return lax.broadcasted_iota(jnp.int32, shape, 0)


def in_layer(tiles):
    blocks, chunks = len(tiles), len(tiles[0])
    lane, sub = lanes_of(), subs_of()
    zero = jnp.zeros((SUB, LANES), jnp.float32)
    before = [[pltpu.roll(t, 1, 1) for t in row] for row in tiles]
    after = [[pltpu.roll(t, LANES - 1, 1) for t in row] for row in tiles]
    above = [[pltpu.roll(t, 1, 0) for t in row] for row in tiles]
    below = [[pltpu.roll(t, SUB - 1, 0) for t in row] for row in tiles]
    out = []
    for b in range(blocks):
        row = []
        for c in range(chunks):
            west = jnp.where(lane == 0, before[b][c - 1] if c else zero, before[b][c])
            east = jnp.where(lane == LANES - 1, after[b][c + 1] if c + 1 < chunks else zero, after[b][c])
            north = jnp.where(sub == 0, above[b - 1][c] if b else zero, above[b][c])
            south = jnp.where(sub == SUB - 1, below[b + 1][c] if b + 1 < blocks else zero, below[b][c])
            row.append((west + east) + (north + south))
        out.append(row)
    return out


def load(ref, at, blocks, chunks):
    return [[ref[pl.ds(at + SUB * b, SUB), c * LANES:(c + 1) * LANES] for c in range(chunks)] for b in range(blocks)]


def store(ref, at, tiles):
    for b, row in enumerate(tiles):
        for c, tile in enumerate(row):
            ref[pl.ds(at + SUB * b, SUB), c * LANES:(c + 1) * LANES] = tile


def total(*terms):
    terms = [t for t in terms if t is not None]
    out = []
    for b in range(len(terms[0])):
        row = []
        for c in range(len(terms[0][0])):
            value = terms[0][b][c]
            for t in terms[1:]:
                value = value + t[b][c]
            row.append(value * SIXTH)
        out.append(row)
    return out


def spread(tile, i):
    return jnp.broadcast_to(tile[i:i + 1, :], (SUB, LANES))


def stack(rows):
    sub = subs_of()
    out = []
    for c in range(len(rows[0])):
        value = rows[0][c]
        for i in range(1, len(rows)):
            value = jnp.where(sub == i, rows[i][c], value)
        out.append(value)
    return out


def near_row(right, first, last, m):
    return [jnp.where(right, spread(f, m), spread(t, SUB - 1 - m)) for f, t in zip(first, last)]


def face_kernel(info, phi, src, pack_a, pack_b, pack_y, diag_a, diag_b, p0, s0, ps, edge0, edge_s, edge, sem):
    cz, cy, nx = phi.shape
    blocks, chunks = cy // SUB, nx // LANES
    odd, col = info[0], info[1]
    right = (col == 1)
    copies = []
    for i in range(2):
        low = odd if i == 0 else 1 - odd
        for j in range(4):
            z = jnp.where(low == 1, j, cz - 1 - j)
            copies.append(pltpu.make_async_copy(phi.at[z], p0.at[i, j], sem.at[i, j]))
            if j < 3:
                copies.append(pltpu.make_async_copy(src.at[z], s0.at[i, j], sem.at[i, 4 + j]))
    at = pl.multiple_of(jnp.where(right, 0, cy - SUB), SUB)
    edges = [
        pltpu.make_async_copy(phi.at[:, pl.ds(at, SUB), :], edge0, sem.at[0, 7]),
        pltpu.make_async_copy(src.at[:, pl.ds(at, SUB), :], edge_s, sem.at[1, 7]),
    ]
    for c in copies + edges:
        c.start()
    for c in copies:
        c.wait()
    for i, (pack, diag) in enumerate(((pack_a, diag_a), (pack_b, diag_b))):
        layer0 = [load(p0.at[i, j], 0, blocks, chunks) for j in range(4)]
        layer_s = [load(s0.at[i, j], 0, blocks, chunks) for j in range(3)]
        store(pack, 0, layer0[0])
        layer1 = []
        for j in range(3):
            layer1.append(total(layer_s[j], in_layer(layer0[j]), layer0[j + 1], layer0[j - 1] if j else None))
            if j:
                store(ps.at[i, j - 1], 0, layer1[j])
            else:
                store(pack, cy, layer1[j])
        layer1 = [load(pack, cy, blocks, chunks)] + [load(ps.at[i, j], 0, blocks, chunks) for j in range(2)]
        layer2 = []
        for j in range(2):
            layer2.append(total(layer_s[j], in_layer(layer1[j]), layer1[j + 1], layer1[j - 1] if j else None))
            if j:
                store(ps.at[i, 2], 0, layer2[j])
            else:
                store(pack, 2 * cy, layer2[j])
        layer2 = [load(pack, 2 * cy, blocks, chunks), load(ps.at[i, 2], 0, blocks, chunks)]
        store(pack, 3 * cy, total(layer_s[0], in_layer(layer2[0]), layer2[1]))
        near = lambda layer, m: near_row(right, layer[0], layer[-1], m)
        store(pack, 4 * cy, [near(layer0[1], 0)])
        store(pack_y, 4 * cz, [stack([near(layer0[0], 1)] * 2)]) if i == 0 else None
        if i == 1:
            kept = load(pack_y, 4 * cz, 1, chunks)[0]
            store(pack_y, 4 * cz, [stack([kept, near(layer0[0], 1)])])
        first = [near(layer0[0], 0), near(layer0[1], 0), near(layer0[2], 0), near(layer1[0], 0), near(layer1[1], 0),
                 near(layer2[0], 0), near(layer0[0], 1), near(layer0[0], 2)]
        store(diag, 0, [stack(first)])
        store(diag, SUB, [near(layer1[0], 1)])
    for c in edges:
        c.wait()

    def planes(k, tiles):
        for half in range(cz // SUB):
            rows = [near_row(right, tiles[half * SUB + z], tiles[half * SUB + z], 0) for z in range(SUB)]
            store(pack_y, k * cz + half * SUB, [stack(rows)])

    now = [[edge0[z, :, c * LANES:(c + 1) * LANES] for c in range(chunks)] for z in range(cz)]
    planes(0, now)
    for k in range(1, 4):
        then = []
        for z in range(cz):
            source = [[edge_s[z, :, c * LANES:(c + 1) * LANES] for c in range(chunks)]]
            parts = [source, in_layer([now[z]])]
            if z:
                parts.append([now[z - 1]])
            if z + 1 < cz:
                parts.append([now[z + 1]])
            tiles = total(*parts)
            then.append(tiles[0])
            for c in range(chunks):
                edge[k % 2, z, :, c * LANES:(c + 1) * LANES] = tiles[0][c]
        now = [[edge[k % 2, z, :, c * LANES:(c + 1) * LANES] for c in range(chunks)] for z in range(cz)]
        planes(k, now)


def faces(info, phi, src):
    cz, cy, nx = phi.shape
    f32 = lambda *shape: jax.ShapeDtypeStruct(shape, jnp.float32)
    return pl.pallas_call(
        face_kernel,
        out_shape=(f32(4 * cy + SUB, nx), f32(4 * cy + SUB, nx), f32(4 * cz + SUB, nx), f32(2 * SUB, nx), f32(2 * SUB, nx)),
        in_specs=[SMEM, ANY, ANY],
        out_specs=(VMEM,) * 5,
        scratch_shapes=[
            pltpu.VMEM((2, 4, cy, nx), jnp.float32),
            pltpu.VMEM((2, 3, cy, nx), jnp.float32),
            pltpu.VMEM((2, 3, cy, nx), jnp.float32),
            pltpu.VMEM((cz, SUB, nx), jnp.float32),
            pltpu.VMEM((cz, SUB, nx), jnp.float32),
            pltpu.VMEM((2, cz, SUB, nx), jnp.float32),
            pltpu.SemaphoreType.DMA((2, 8)),
        ],
        compiler_params=pltpu.CompilerParams(vmem_limit_bytes=24 << 20),
        name="faces",
    )(info, phi, src)


def alone_kernel(phi, src, out, buf, sources, sem):
    cz, cy, nx = phi.shape
    blocks, chunks = cy // SUB, nx // LANES
    copies = [
        pltpu.make_async_copy(phi, buf.at[0, 1:cz + 1], sem.at[0]),
        pltpu.make_async_copy(src, sources, sem.at[1]),
    ]
    for c in copies:
        c.start()
    zero = [[jnp.zeros((SUB, LANES), jnp.float32)] * chunks] * blocks
    for i in range(2):
        for z in (0, cz + 1):
            store(buf.at[i, z], 0, zero)
    for c in copies:
        c.wait()

    for k in range(ITERS):
        last = k == ITERS - 1

        def layer(z, carry, k=k, last=last):
            at = k % 2
            value = total(
                load(sources.at[z], 0, blocks, chunks),
                in_layer(load(buf.at[at, z + 1], 0, blocks, chunks)),
                load(buf.at[at, z], 0, blocks, chunks),
                load(buf.at[at, z + 2], 0, blocks, chunks),
            )
            if last:
                for c in range(chunks):
                    for b in range(blocks):
                        out[c, pl.ds(pl.multiple_of(z * cy, SUB) + SUB * b, SUB), :] = value[b][c]
            else:
                store(buf.at[1 - at, z + 1], 0, value)
            return carry

        lax.fori_loop(0, cz, layer, 0)


def alone(phi, src):
    cz, cy, nx = phi.shape
    return pl.pallas_call(
        alone_kernel,
        out_shape=jax.ShapeDtypeStruct((nx // LANES, cz * cy, LANES), jnp.float32),
        in_specs=[ANY, ANY],
        out_specs=VMEM,
        scratch_shapes=[
            pltpu.VMEM((2, cz + 2, cy, nx), jnp.float32),
            pltpu.VMEM((cz, cy, nx), jnp.float32),
            pltpu.SemaphoreType.DMA((2,)),
        ],
        compiler_params=pltpu.CompilerParams(vmem_limit_bytes=24 << 20),
        cost_estimate=pl.CostEstimate(flops=10 * ITERS * phi.size, bytes_accessed=12 * phi.size, transcendentals=0),
        name="alone",
    )(phi, src)


def respond(blocks, chunks, outer, inner, mask, scratch, finish):
    slot = iter(range(scratch.shape[0]))

    def keep(tiles):
        ref = scratch.at[next(slot)]
        store(ref, 0, mask(tiles))
        return lambda: load(ref, 0, blocks, chunks)

    o0, i0 = keep(total(outer(0))), keep(total(inner(0)))
    o0_2 = keep(total(outer(1), in_layer(o0()), i0()))
    i0_2 = keep(total(inner(1), in_layer(i0()), o0()))
    o1_2, i1_2 = keep(total(o0())), keep(total(i0()))
    o0_3 = keep(total(outer(2), in_layer(o0_2()), o1_2(), i0_2()))
    i0_3 = keep(total(inner(2), in_layer(i0_2()), o0_2(), i1_2()))
    i1_3 = keep(total(in_layer(i1_2()), i0_2()))
    i2_3 = keep(total(i1_2()))
    finish(0, total(inner(3), in_layer(i0_3()), o0_3(), i1_3()))
    finish(1, total(in_layer(i1_3()), i0_3(), i2_3()))
    finish(2, total(in_layer(i2_3()), i1_3()))
    finish(3, total(i2_3()))


SLOTS = 10


def join_kernel(
    info, row_of, lane_of, block, own_a, own_b, own_y, got_a, got_b, got_y, got_da, got_db,
    potential, values, pot, layers, columns, picked, sem,
):
    chunks, cells, _ = pot.shape
    cy = (own_a.shape[0] - SUB) // 4
    cz = cells // cy
    blocks = cy // SUB
    odd, right = info[0], info[1] == 1
    has = (info[2].astype(jnp.float32), info[3].astype(jnp.float32))
    fetch = pltpu.make_async_copy(block, pot, sem.at[0])
    fetch.start()
    sub = subs_of()
    zero = [jnp.zeros((SUB, LANES), jnp.float32)] * chunks
    at_low = jnp.where(right, 1.0, 0.0)
    at_high = 1.0 - at_low

    def tile_row(ref, at):
        return load(ref, at, 1, chunks)[0]

    def row(ref, at, i):
        return [spread(t, i) for t in tile_row(ref, at)]

    def scale(tiles, factor):
        return [t * factor for t in tiles]

    def flank(rows, low):
        if not rows:
            return zero
        out = zero
        for m, value in enumerate(rows):
            out = [jnp.where(sub == (SUB - 1 - m if low else m), v, o) for v, o in zip(value, out)]
        return out

    def near(ref, at, m):
        return near_row(right, tile_row(ref, at), tile_row(ref, at + cy - SUB), m)

    def diag(ref, k, j=0, m=0):
        place = {(0, 0, 0): 0, (0, 1, 0): 1, (0, 2, 0): 2, (1, 0, 0): 3, (1, 1, 0): 4, (2, 0, 0): 5, (0, 0, 1): 6,
                 (0, 0, 2): 7, (1, 0, 1): 8}[(k, j, m)]
        return row(ref, place // SUB * SUB, place % SUB)

    for i, (own, got, got_d) in enumerate(((own_a, got_a, got_da), (own_b, got_b, got_db))):
        low_side = odd if i == 0 else 1 - odd

        def layer_start(j, low_side=low_side):
            return pl.multiple_of(jnp.where(low_side == 1, j, cz - 1 - j) * cy, SUB)

        def column_row(ref, k, low_side=low_side):
            return [jnp.where(low_side == 1, a, b) for a, b in zip(row(ref, k * cz, 0), row(ref, k * cz + cz - SUB, SUB - 1))]

        def driven(plane, rows, i=i):
            middle = [scale(t, has[i]) for t in plane]
            return ([scale(flank(rows, True), has[i] * at_low)] + middle + [scale(flank(rows, False), has[i] * at_high)])

        def inner(k, got=got, got_d=got_d, driven=driven):
            rows = [diag(got_d, k, m=m) for m in range(3 - k)]
            return driven(load(got, k * cy, blocks, chunks), rows)

        def outer(k, own=own, driven=driven, column_row=column_row, i=i):
            rows = [column_row(got_y, k)] if k < 2 else []
            if k == 0:
                rows.append(row(got_y, 4 * cz, i))
            return driven(load(own, k * cy, blocks, chunks), rows)

        def mask(tiles):
            return [scale(tiles[0], at_low)] + tiles[1:-1] + [scale(tiles[-1], at_high)]

        def finish(j, tiles, i=i, layer_start=layer_start):
            if i == 0 and j == 0:
                fetch.wait()
            start = layer_start(j)
            for b in range(blocks):
                for c in range(chunks):
                    where = (c, pl.ds(start + SUB * b, SUB), slice(None))
                    pot[where] = pot[where] + tiles[b + 1][c]

        respond(blocks + 2, chunks, outer, inner, mask, layers, finish)

    low_has = jnp.where(odd == 1, has[0], has[1])
    high_has = jnp.where(odd == 1, has[1], has[0])

    def either(a, b):
        return [jnp.where(odd == 1, x, y) for x, y in zip(a, b)], [jnp.where(odd == 1, y, x) for x, y in zip(a, b)]

    def along(plane, pairs):
        low = scale(flank([p[0] for p in pairs], True), low_has)
        high = scale(flank([p[1] for p in pairs], False), high_has)
        return [low] + plane + [high]

    def inner_y(k):
        pairs = [either(diag(got_da, k, j=j), diag(got_db, k, j=j)) for j in range(3 - k)]
        return along(load(got_y, k * cz, cz // SUB, chunks), pairs)

    def outer_y(k):
        pairs = [either(near(got_a, k * cy, 0), near(got_b, k * cy, 0))] if k < 2 else []
        if k == 0:
            pairs.append(either(row(got_a, 4 * cy, 0), row(got_b, 4 * cy, 0)))
        return along(load(own_y, k * cz, cz // SUB, chunks), pairs)

    def mask_y(tiles):
        return [scale(tiles[0], low_has)] + tiles[1:-1] + [scale(tiles[-1], high_has)]

    ends = []

    def finish_y(j, tiles):
        ends.append(tiles[1:-1])

    respond(cz // SUB + 2, chunks, outer_y, inner_y, mask_y, columns, finish_y)
    edge = pl.multiple_of(jnp.where(right, 0, cy - SUB), SUB)
    for z in range(cz):
        for c in range(chunks):
            change = jnp.zeros((SUB, LANES), jnp.float32)
            for m in range(4):
                place = jnp.where(right, m, SUB - 1 - m)
                change = jnp.where(sub == place, spread(ends[m][z // SUB][c], z % SUB), change)
            where = (c, pl.ds(z * cy + edge, SUB), slice(None))
            pot[where] = pot[where] + change

    leave = [
        pltpu.make_async_copy(pot.at[c], potential.at[:, pl.ds(c * LANES, LANES)], sem.at[1 + c]) for c in range(chunks)
    ]
    for c in leave:
        c.start()

    flat = pot.reshape(chunks * cells, LANES)
    wide = picked.shape[0]

    def pick(g, carry):
        for u in range(16):
            i = g * 16 + u
            picked[pl.ds(i, 1), :] = flat[pl.ds(row_of[i], 1), :]
        return carry

    lax.fori_loop(0, wide // 16, pick, 0)
    deep = lax.broadcasted_iota(jnp.int32, (LANES, LANES), 0)
    for q in range(wide // LANES):
        turned = picked[q * LANES:(q + 1) * LANES, :].T
        chosen = jnp.where(deep == lane_of[q:q + 1, :], turned, 0.0)
        line = jnp.sum(chosen, axis=0, keepdims=True)
        values[:, :, q * LANES:(q + 1) * LANES] = jnp.broadcast_to(line[None], (values.shape[0], 1, LANES))
    for c in leave:
        c.wait()


def join(info, row_of, lane_of, block, own, got, devices):
    chunks, cells, _ = block.shape
    cy = (own[0].shape[0] - SUB) // 4
    cz = cells // cy
    nodes = row_of.shape[0]
    nx = chunks * LANES
    return pl.pallas_call(
        join_kernel,
        out_shape=(
            jax.ShapeDtypeStruct((cells, nx), jnp.float32),
            jax.ShapeDtypeStruct((devices, 1, nodes), jnp.float32),
        ),
        in_specs=[SMEM, SMEM, VMEM, ANY] + [VMEM] * 8,
        out_specs=(ANY, VMEM),
        scratch_shapes=[
            pltpu.VMEM((chunks, cells, LANES), jnp.float32),
            pltpu.VMEM((SLOTS, cy + 2 * SUB, nx), jnp.float32),
            pltpu.VMEM((SLOTS, cz + 2 * SUB, nx), jnp.float32),
            pltpu.VMEM((nodes, LANES), jnp.float32),
            pltpu.SemaphoreType.DMA((1 + chunks,)),
        ],
        compiler_params=pltpu.CompilerParams(vmem_limit_bytes=24 << 20),
        name="join",
    )(info, row_of, lane_of, block, *own[:3], *got)


def window_kernel(col_ref, table_ref, slot_ref, matrix_hbm, keep_ref, send_ref, matrix_ref, trace_ref, sem):
    copy = pltpu.make_async_copy(matrix_hbm, matrix_ref, sem)
    copy.start()
    owners, _, width = table_ref.shape
    parts = width // LANES
    chunks = trace_ref.shape[0]
    group = 12
    first = col_ref[0] * chunks

    def gather_group(g, carry):
        base = pl.multiple_of(g * (group * SUB), SUB)
        slots = [slot_ref[pl.ds(pl.multiple_of(first + base + SUB * v, SUB), SUB), :] for v in range(group)]
        low = [s & (LANES - 1) for s in slots]
        high = [s >> 7 for s in slots]

        def owner_step(d, accs):
            accs = list(accs)
            for q in range(parts):
                row = jnp.broadcast_to(table_ref[d, :, q * LANES:(q + 1) * LANES], (SUB, LANES))
                number = d * parts + q
                for v in range(group):
                    picked = jnp.take_along_axis(row, low[v], axis=1)
                    accs[v] = jnp.where(high[v] == number, picked, accs[v])
            return tuple(accs)

        zero = jnp.zeros((SUB, LANES), jnp.float32)
        accs = lax.fori_loop(0, owners, owner_step, (zero,) * group)
        for v in range(group):
            trace_ref[pl.ds(pl.multiple_of(base + SUB * v, SUB), SUB), :] = accs[v]
        return carry

    lax.fori_loop(0, chunks // (SUB * group), gather_group, 0)
    copy.wait()
    rows = matrix_ref.shape[0]
    blocks = rows // 16
    start = [pl.multiple_of(col_ref[0] * (rows // 2), SUB), pl.multiple_of((1 - col_ref[0]) * (rows // 2), SUB)]

    def chunk_step(c, accs):
        accs = list(accs)
        for u in range(SUB):
            at = pl.multiple_of((c * SUB + u) * LANES, LANES)
            value = jnp.broadcast_to(trace_ref[pl.ds(c * SUB + u, 1), :], (SUB, LANES))
            for side in range(2):
                for b in range(blocks):
                    tile = matrix_ref[pl.ds(start[side] + SUB * b, SUB), pl.ds(at, LANES)]
                    accs[side * blocks + b] = accs[side * blocks + b] + tile * value
        return tuple(accs)

    zero = jnp.zeros((SUB, LANES), jnp.float32)
    accs = lax.fori_loop(0, chunks // SUB, chunk_step, (zero,) * (2 * blocks))
    for side, out in enumerate((keep_ref, send_ref)):
        tall = jnp.concatenate(accs[side * blocks:(side + 1) * blocks] + (zero,) * (16 - blocks), axis=0)
        out[...] = jnp.sum(tall.T, axis=0, keepdims=True)


def window_product(col, table, slots, matrix):
    rows, columns = matrix.shape
    chunks = columns // LANES
    out = jax.ShapeDtypeStruct((1, LANES), jnp.float32)
    return pl.pallas_call(
        window_kernel,
        out_shape=(out, out),
        in_specs=[SMEM, VMEM, VMEM, pl.BlockSpec(memory_space=pltpu.HBM)],
        out_specs=(VMEM, VMEM),
        scratch_shapes=[
            pltpu.VMEM((rows, columns), jnp.float32),
            pltpu.VMEM((chunks, LANES), jnp.float32),
            pltpu.SemaphoreType.DMA,
        ],
        compiler_params=pltpu.CompilerParams(vmem_limit_bytes=48 << 20),
        name="window",
    )(col, table, slots, matrix)


def routes(n):
    def across(r):
        other = r + 1 if r % 2 else r - 1
        return other if 0 <= other < n else None

    near = [(r, r ^ 1) for r in range(n)]
    far, near_diag, far_diag = [], [], []
    for r in range(n):
        for c in range(2):
            other = across(r)
            far.append((r * 2 + c, r * 2 + 1 - c if other is None else other * 2 + c))
            near_diag.append((r * 2 + c, (r ^ 1) * 2 + 1 - c))
            far_diag.append((r * 2 + c, (r if other is None else other) * 2 + 1 - c))
    return near, far, near_diag, far_diag


def local(phi_start, source, owner_voxel, column_slot, layer_matrix):
    n = lax.axis_size("rows")
    assert lax.axis_size("cols") == 2 and n % 2 == 0
    devices = 2 * n
    cz, cy, nx = phi_start.shape
    r = lax.axis_index("rows").astype(jnp.int32)
    col = lax.axis_index("cols").astype(jnp.int32)
    odd = r % 2
    far_row = jnp.where(odd == 1, r < n - 1, r > 0).astype(jnp.int32)
    info = jnp.stack([odd, col, jnp.ones_like(odd), far_row])
    near, far, near_diag, far_diag = routes(n)
    swap = [(0, 1), (1, 0)]

    pack_a, pack_b, pack_y, diag_a, diag_b = faces(info, phi_start, source)
    got_b = lax.ppermute(pack_b, BOTH, far)
    got_db = lax.ppermute(diag_b, BOTH, far_diag)
    got_y = lax.ppermute(pack_y, "cols", swap)
    got_da = lax.ppermute(diag_a, BOTH, near_diag)
    got_a = lax.ppermute(pack_a, "rows", near)
    block = alone(phi_start, source)
    x = owner_voxel % nx
    row_of = (x // LANES) * (cz * cy) + owner_voxel // nx
    lane_of = (x % LANES).reshape(-1, LANES)
    potential, values = join(
        info, row_of, lane_of, block, (pack_a, pack_b, pack_y), (got_a, got_b, got_y, got_da, got_db), devices
    )
    table = lax.all_to_all(values, BOTH, 0, 0, tiled=True)
    slots = column_slot.reshape(-1, LANES)
    keep, send = window_product(col[None], table, slots, layer_matrix)
    received = lax.ppermute(send, "cols", swap)
    half = layer_matrix.shape[0] // 2
    return potential.reshape(cz, cy, nx), (keep + received)[0, :half]


def solution(mesh):
    return jax.shard_map(
        local,
        mesh=mesh,
        in_specs=(
            P("rows", "cols", None),
            P("rows", "cols", None),
            P(("rows", "cols")),
            P(),
            P("rows", "cols"),
        ),
        out_specs=(P("rows", "cols", None), P(("rows", "cols"))),
        check_vma=False,
    )
```

```python
import functools

import jax
import jax.numpy as jnp
from jax import lax
from jax.experimental import pallas as pl
from jax.experimental.pallas import tpu as pltpu
from jax.sharding import PartitionSpec as P

ITERS = 4
LANES = 128
SUB = 8
SIXTH = 1.0 / 6.0
FIRST_LIMIT = 58 << 20
BOTH = ("rows", "cols")
VMEM = pl.BlockSpec(memory_space=pltpu.VMEM)
SMEM = pl.BlockSpec(memory_space=pltpu.SMEM)
ANY = pl.BlockSpec(memory_space=pl.ANY)


def lanes_of(shape=(SUB, LANES)):
    return lax.broadcasted_iota(jnp.int32, shape, 1)


def subs_of(shape=(SUB, LANES)):
    return lax.broadcasted_iota(jnp.int32, shape, 0)


PAD = SUB


def around(ref, slot, rows):
    chunks = ref.shape[1]
    lane = lanes_of()
    zero = jnp.zeros((SUB, LANES), jnp.float32)
    out = []
    for b in range(rows // SUB):
        at = PAD + SUB * b
        here = [ref[slot, c, pl.ds(at, SUB), :] for c in range(chunks)]
        before = [pltpu.roll(t, 1, 1) for t in here]
        after = [pltpu.roll(t, LANES - 1, 1) for t in here]
        row = []
        for c in range(chunks):
            west = jnp.where(lane == 0, before[c - 1] if c else zero, before[c])
            east = jnp.where(lane == LANES - 1, after[c + 1] if c + 1 < chunks else zero, after[c])
            row.append((west + east) + (ref[slot, c, pl.ds(at - 1, SUB), :] + ref[slot, c, pl.ds(at + 1, SUB), :]))
        out.append(row)
    return out


def layer_of(ref, slot, rows):
    return [[ref[slot, c, pl.ds(PAD + SUB * b, SUB), :] for c in range(ref.shape[1])] for b in range(rows // SUB)]


def keep_layer(ref, slot, tiles):
    for b, row in enumerate(tiles):
        for c, tile in enumerate(row):
            ref[slot, c, pl.ds(PAD + SUB * b, SUB), :] = tile


def clear_pads(ref, slot, rows):
    zero = jnp.zeros((SUB, LANES), jnp.float32)
    for c in range(ref.shape[1]):
        ref[slot, c, 0:PAD, :] = zero
        ref[slot, c, PAD + rows:2 * PAD + rows, :] = zero


def load(ref, at, blocks):
    return [[ref[c, pl.ds(at + SUB * b, SUB), :] for c in range(ref.shape[0])] for b in range(blocks)]


def store(ref, at, tiles):
    for b, row in enumerate(tiles):
        for c, tile in enumerate(row):
            ref[c, pl.ds(at + SUB * b, SUB), :] = tile


def total(*terms):
    terms = [t for t in terms if t is not None]
    out = []
    for b in range(len(terms[0])):
        row = []
        for c in range(len(terms[0][0])):
            value = terms[0][b][c]
            for t in terms[1:]:
                value = value + t[b][c]
            row.append(value * SIXTH)
        out.append(row)
    return out


def spread(tile, i):
    return jnp.broadcast_to(tile[i:i + 1, :], (SUB, LANES))


def stack(rows):
    sub = subs_of()
    out = []
    for c in range(len(rows[0])):
        value = rows[0][c]
        for i in range(1, len(rows)):
            value = jnp.where(sub == i, rows[i][c], value)
        out.append(value)
    return out


def near_row(right, first, last, m):
    return [jnp.where(right, spread(f, m), spread(t, SUB - 1 - m)) for f, t in zip(first, last)]


def solve_face(first, source, work, pack, rows):
    blocks = rows // SUB
    start = [layer_of(*first(j), rows) for j in range(4)]
    store(pack, 0, start[0])
    for j in range(3):
        keep_layer(work, j, total(source(j), around(*first(j), rows), start[j + 1], start[j - 1] if j else None))
    one = [layer_of(work, j, rows) for j in range(3)]
    store(pack, rows, one[0])
    for j in range(2):
        keep_layer(work, 3 + j, total(source(j), around(work, j, rows), one[j + 1], one[j - 1] if j else None))
    two = [layer_of(work, 3 + j, rows) for j in range(2)]
    store(pack, 2 * rows, two[0])
    store(pack, 3 * rows, total(source(0), around(work, 3, rows), two[1]))


def fetch_face(phi, src, low, raw, sem):
    last = phi.shape[0] - 1
    copies = []
    for j in range(4):
        z = jnp.where(low == 1, j, last - j)
        copies.append(pltpu.make_async_copy(phi.at[z], raw.at[0, j], sem.at[0, j]))
        if j < 3:
            copies.append(pltpu.make_async_copy(src.at[z], raw.at[1, j], sem.at[1, j]))
    return copies


def tiles_of(ref):
    rows, wide = ref.shape
    return [[ref[SUB * b:SUB * b + SUB, c * LANES:(c + 1) * LANES] for c in range(wide // LANES)] for b in range(rows // SUB)]


def send_face(right, source, p0, work, pack, diag, cy):
    chunks = p0.shape[1]
    solve_face(lambda j: (p0, j), source, work, pack, cy)

    def near(ref, slot, m):
        edges = [[ref[slot, c, pl.ds(at, SUB), :] for c in range(chunks)] for at in (PAD, PAD + cy - SUB)]
        return near_row(right, *edges, m)

    store(pack, 4 * cy, [near(p0, 1, 0)])
    store(diag, 0, [stack([
        near(p0, 0, 0), near(p0, 1, 0), near(p0, 2, 0), near(work, 0, 0), near(work, 1, 0),
        near(work, 3, 0), near(p0, 0, 1), near(p0, 0, 2),
    ])])
    store(diag, SUB, [near(work, 0, 1)])


def far_face_kernel(phi, src, pack, diag, raw, p0, work, sem):
    cy = phi.shape[1]
    odd, col, _ = whereabouts()
    copies = fetch_face(phi, src, 1 - odd, raw, sem)
    for c in copies:
        c.start()
    for i in range(4):
        clear_pads(p0, i, cy)
    for i in range(5):
        clear_pads(work, i, cy)
    for c in copies:
        c.wait()
    for j in range(4):
        keep_layer(p0, j, tiles_of(raw.at[0, j]))
    send_face(col == 1, lambda j: tiles_of(raw.at[1, j]), p0, work, pack, diag, cy)


def f32(*shape):
    return jax.ShapeDtypeStruct(shape, jnp.float32)


def face_scratch(chunks, cy):
    tall = cy + 2 * PAD
    return [
        pltpu.VMEM((2, 4, cy, chunks * LANES), jnp.float32),
        pltpu.VMEM((4, chunks, tall, LANES), jnp.float32),
        pltpu.VMEM((5, chunks, tall, LANES), jnp.float32),
    ]


def whereabouts():
    n, r = lax.axis_size("rows"), lax.axis_index("rows").astype(jnp.int32)
    odd = lax.rem(r, 2)
    return odd, lax.axis_index("cols").astype(jnp.int32), jnp.where(odd == 1, r < n - 1, r > 0).astype(jnp.int32)


def far_face(phi, src):
    cz, cy, nx = phi.shape
    chunks = nx // LANES
    return pl.pallas_call(
        far_face_kernel,
        out_shape=(f32(chunks, 4 * cy + SUB, LANES), f32(chunks, 2 * SUB, LANES)),
        in_specs=[ANY, ANY],
        out_specs=(VMEM, VMEM),
        scratch_shapes=face_scratch(chunks, cy) + [pltpu.SemaphoreType.DMA((2, 4))],
        compiler_params=pltpu.CompilerParams(vmem_limit_bytes=FIRST_LIMIT),
        name="far_face",
    )(phi, src)


def near_face_kernel(after, phi, src, pack, pack_y, diag, p0, work, edge, edge_p, edge_w):
    cz, cy, nx = phi.shape
    chunks = nx // LANES
    odd, col, _ = whereabouts()
    right = col == 1
    for i in range(4):
        clear_pads(p0, i, cy)
        clear_pads(edge_p, i, cz)
    for i in range(5):
        clear_pads(work, i, cy)
        clear_pads(edge_w, i, cz)

    def layer(j):
        return jnp.where(odd == 1, j, cz - 1 - j)

    for j in range(4):
        keep_layer(p0, j, tiles_of(phi.at[layer(j)]))
    send_face(right, lambda j: tiles_of(src.at[layer(j)]), p0, work, pack, diag, cy)
    at = pl.multiple_of(jnp.where(right, 0, cy - SUB), SUB)
    for i, whole in enumerate((phi, src)):
        for z in range(cz):
            for c in range(chunks):
                edge[i, c, z * SUB:(z + 1) * SUB, :] = whole[z, pl.ds(at, SUB), c * LANES:(c + 1) * LANES]
    flat = edge.reshape(2 * chunks * cz * SUB, LANES)

    def plane(i, c, m):
        row = jnp.where(right, m, SUB - 1 - m)
        return flat[pl.ds((i * chunks + c) * cz * SUB + row, cz, stride=SUB), :]

    for m in range(4):
        for c in range(chunks):
            edge_p[m, c, PAD:PAD + cz, :] = plane(0, c, m)

    def source(m):
        whole = [plane(1, c, m) for c in range(chunks)]
        return [[w[SUB * b:SUB * b + SUB, :] for w in whole] for b in range(cz // SUB)]

    solve_face(lambda j: (edge_p, j), source, edge_w, pack_y, cz)
    ends = [[edge_p[1, c, pl.ds(PAD + i, 1), :] for c in range(chunks)] for i in (0, cz - 1)]
    ends = [[jnp.broadcast_to(t, (SUB, LANES)) for t in row] for row in ends]
    own = [[jnp.where(odd == 1, a, b) for a, b in zip(*ends)], [jnp.where(odd == 1, b, a) for a, b in zip(*ends)]]
    store(pack_y, 4 * cz, [stack(own)])


def near_face(after, phi, src):
    cz, cy, nx = phi.shape
    chunks = nx // LANES
    tall = cz + 2 * PAD
    return pl.pallas_call(
        near_face_kernel,
        out_shape=(f32(chunks, 4 * cy + SUB, LANES), f32(chunks, 4 * cz + SUB, LANES), f32(chunks, 2 * SUB, LANES)),
        in_specs=[ANY, VMEM, VMEM],
        out_specs=(VMEM,) * 3,
        scratch_shapes=face_scratch(chunks, cy)[1:] + [
            pltpu.VMEM((2, chunks, cz * SUB, LANES), jnp.float32),
            pltpu.VMEM((4, chunks, tall, LANES), jnp.float32),
            pltpu.VMEM((5, chunks, tall, LANES), jnp.float32),
        ],
        compiler_params=pltpu.CompilerParams(vmem_limit_bytes=24 << 20),
        name="near_face",
    )(after, phi, src)


def alone_kernel(phi, src, matrix, out, matrix_out, buf_a, buf_b, sem):
    cz, cy, nx = phi.shape
    blocks, chunks = cy // SUB, nx // LANES
    pieces = 4
    deep = matrix.shape[0] // pieces
    copies = [
        pltpu.make_async_copy(matrix.at[i * deep:(i + 1) * deep], matrix_out.at[i * deep:(i + 1) * deep], sem.at[i])
        for i in range(pieces)
    ]
    for c in copies:
        c.start()
    zero = [[jnp.zeros((SUB, LANES), jnp.float32)] * chunks] * blocks
    for ref in (buf_a, buf_b):
        for z in (0, cz + 1):
            keep_layer(ref, z, zero)

    def begin(z, carry):
        for ref in (buf_a, buf_b):
            clear_pads(ref, z + 1, cy)
        keep_layer(buf_a, z + 1, tiles_of(phi.at[z]))
        return carry

    lax.fori_loop(0, cz, begin, 0)
    for k in range(ITERS):
        here, there = (buf_a, buf_b) if k % 2 == 0 else (buf_b, buf_a)

        def layer(z, carry, here=here, there=there, last=k == ITERS - 1):
            value = total(tiles_of(src.at[z]), around(here, z + 1, cy), layer_of(here, z, cy), layer_of(here, z + 2, cy))
            if last:
                for c in range(chunks):
                    for b in range(blocks):
                        out[c, pl.ds(pl.multiple_of(z * cy, SUB) + SUB * b, SUB), :] = value[b][c]
            else:
                keep_layer(there, z + 1, value)
            return carry

        lax.fori_loop(0, cz, layer, 0)
    for c in copies:
        c.wait()


def alone(phi, src, matrix):
    cz, cy, nx = phi.shape
    chunks = nx // LANES
    return pl.pallas_call(
        alone_kernel,
        out_shape=(f32(chunks, cz * cy, LANES), f32(*matrix.shape)),
        in_specs=[VMEM, VMEM, ANY],
        out_specs=(VMEM, VMEM),
        scratch_shapes=[
            pltpu.VMEM((cz + 2, chunks, cy + 2 * PAD, LANES), jnp.float32),
            pltpu.VMEM((cz + 2, chunks, cy + 2 * PAD, LANES), jnp.float32),
            pltpu.SemaphoreType.DMA((4,)),
        ],
        compiler_params=pltpu.CompilerParams(vmem_limit_bytes=40 << 20),
        cost_estimate=pl.CostEstimate(flops=10 * ITERS * phi.size, bytes_accessed=12 * phi.size, transcendentals=0),
        name="alone",
    )(phi, src, matrix)


def respond(rows, outer, inner, mask, work, finish):
    for slot in range(SLOTS):
        clear_pads(work, slot, rows)
    o0, i0, o0_2, i0_2, o1_2, i1_2, o0_3, i0_3, i1_3, i2_3 = range(SLOTS)

    def keep(slot, *terms):
        keep_layer(work, slot, mask(total(*terms)))

    def at(slot):
        return layer_of(work, slot, rows)

    def near(slot):
        return around(work, slot, rows)

    keep(o0, outer(0))
    keep(i0, inner(0))
    keep(o0_2, outer(1), near(o0), at(i0))
    keep(i0_2, inner(1), near(i0), at(o0))
    keep(o1_2, at(o0))
    keep(i1_2, at(i0))
    keep(o0_3, outer(2), near(o0_2), at(o1_2), at(i0_2))
    keep(i0_3, inner(2), near(i0_2), at(o0_2), at(i1_2))
    keep(i1_3, near(i1_2), at(i0_2))
    keep(i2_3, at(i1_2))
    finish(0, total(inner(3), near(i0_3), at(o0_3), at(i1_3)))
    finish(1, total(near(i1_3), at(i0_3), at(i2_3)))
    finish(2, total(near(i2_3), at(i1_3)))
    finish(3, total(at(i2_3)))


SLOTS = 10


class Corner:
    def __init__(self, chunks):
        self.odd, col, has_far = whereabouts()
        self.right = col == 1
        self.has = (1.0, has_far.astype(jnp.float32))
        self.zero = [jnp.zeros((SUB, LANES), jnp.float32)] * chunks
        self.at_low = jnp.where(self.right, 1.0, 0.0)
        self.at_high = 1.0 - self.at_low

    def row(self, ref, at, i):
        return [spread(t, i) for t in load(ref, at, 1)[0]]

    def scale(self, tiles, factor):
        return [t * factor for t in tiles]

    def flank(self, rows, low):
        out, sub = self.zero, subs_of()
        for m, value in enumerate(rows):
            out = [jnp.where(sub == (SUB - 1 - m if low else m), v, o) for v, o in zip(value, out)]
        return out

    def near(self, ref, at, cy, m):
        return near_row(self.right, load(ref, at, 1)[0], load(ref, at + cy - SUB, 1)[0], m)

    def diag(self, ref, k, j=0, m=0):
        place = {(0, 0, 0): 0, (0, 1, 0): 1, (0, 2, 0): 2, (1, 0, 0): 3, (1, 1, 0): 4, (2, 0, 0): 5, (0, 0, 1): 6,
                 (0, 0, 2): 7, (1, 0, 1): 8}[(k, j, m)]
        return self.row(ref, place // SUB * SUB, place % SUB)

    def low_side(self, i):
        return self.odd if i == 0 else 1 - self.odd

    def interface(self, i, own, got, got_d, got_y, cz, cy, work, finish):
        low, blocks = self.low_side(i) == 1, cy // SUB

        def end_row(k):
            return [jnp.where(low, a, b) for a, b in zip(self.row(got_y, k * cz, 0), self.row(got_y, k * cz + cz - SUB, SUB - 1))]

        def driven(plane, rows):
            middle = [self.scale(t, self.has[i]) for t in plane]
            return ([self.scale(self.flank(rows, True), self.has[i] * self.at_low)] + middle
                    + [self.scale(self.flank(rows, False), self.has[i] * self.at_high)])

        def inner(k):
            return driven(load(got, k * cy, blocks), [self.diag(got_d, k, m=m) for m in range(3 - k)])

        def outer(k):
            rows = [end_row(k)] if k < 2 else []
            if k == 0:
                rows.append(self.row(got_y, 4 * cz, i))
            return driven(load(own, k * cy, blocks), rows)

        def mask(tiles):
            return [self.scale(tiles[0], self.at_low)] + tiles[1:-1] + [self.scale(tiles[-1], self.at_high)]

        respond(cy + 2 * SUB, outer, inner, mask, work, lambda j, tiles: finish(j, tiles[1:-1]))


def near_join_kernel(own, got, got_d, got_y, change, work):
    chunks = own.shape[0]
    cy = (own.shape[1] - SUB) // 4
    cz = (got_y.shape[1] - SUB) // 4
    Corner(chunks).interface(0, own, got, got_d, got_y, cz, cy, work, lambda j, tiles: store(change, j * cy, tiles))


def near_join(own, got, got_d, got_y):
    chunks, tall, _ = own.shape
    cy = (tall - SUB) // 4
    return pl.pallas_call(
        near_join_kernel,
        out_shape=f32(chunks, 4 * cy, LANES),
        in_specs=[VMEM] * 4,
        out_specs=VMEM,
        scratch_shapes=[pltpu.VMEM((SLOTS, chunks, cy + 2 * SUB + 2 * PAD, LANES), jnp.float32)],
        compiler_params=pltpu.CompilerParams(vmem_limit_bytes=24 << 20),
        name="near_join",
    )(own, got, got_d, got_y)


def join_kernel(
    row_of, lane_of, block, change, own_b, own_y, got_a, got_b, got_y, got_da, got_db,
    potential, values, pot, layers, columns, picked, sem,
):
    chunks, cells, _ = pot.shape
    cy = (own_b.shape[1] - SUB) // 4
    cz = cells // cy
    blocks = cy // SUB
    place = Corner(chunks)
    odd, right, has = place.odd, place.right, place.has
    fetch = pltpu.make_async_copy(block, pot, sem.at[0])
    fetch.start()
    sub = subs_of()

    def add_layer(i, j, tiles):
        start = pl.multiple_of(jnp.where(place.low_side(i) == 1, j, cz - 1 - j) * cy, SUB)
        for b in range(blocks):
            for c in range(chunks):
                where = (c, pl.ds(start + SUB * b, SUB), slice(None))
                pot[where] = pot[where] + tiles[b][c]

    def finish(j, tiles):
        if j == 0:
            fetch.wait()
            for old in range(4):
                add_layer(0, old, load(change, old * cy, blocks))
        add_layer(1, j, tiles)

    place.interface(1, own_b, got_b, got_db, got_y, cz, cy, layers, finish)

    low_has = jnp.where(odd == 1, has[0], has[1])
    high_has = jnp.where(odd == 1, has[1], has[0])

    def either(a, b):
        return [jnp.where(odd == 1, x, y) for x, y in zip(a, b)], [jnp.where(odd == 1, y, x) for x, y in zip(a, b)]

    def along(plane, pairs):
        low = place.scale(place.flank([p[0] for p in pairs], True), low_has)
        high = place.scale(place.flank([p[1] for p in pairs], False), high_has)
        return [low] + plane + [high]

    def inner_y(k):
        pairs = [either(place.diag(got_da, k, j=j), place.diag(got_db, k, j=j)) for j in range(3 - k)]
        return along(load(got_y, k * cz, cz // SUB), pairs)

    def outer_y(k):
        pairs = [either(place.near(got_a, k * cy, cy, 0), place.near(got_b, k * cy, cy, 0))] if k < 2 else []
        if k == 0:
            pairs.append(either(place.row(got_a, 4 * cy, 0), place.row(got_b, 4 * cy, 0)))
        return along(load(own_y, k * cz, cz // SUB), pairs)

    def mask_y(tiles):
        return [place.scale(tiles[0], low_has)] + tiles[1:-1] + [place.scale(tiles[-1], high_has)]

    flat = pot.reshape(chunks * cells, LANES)

    def finish_y(j, tiles):
        row = jnp.where(right, j, cy - 1 - j)
        for c in range(chunks):
            for half in range(cz // SUB):
                where = (pl.ds(c * cells + half * SUB * cy + row, SUB, stride=cy), slice(None))
                flat[where] = flat[where] + tiles[half + 1][c]

    respond(cz + 2 * SUB, outer_y, inner_y, mask_y, columns, finish_y)

    leave = [
        pltpu.make_async_copy(pot.at[c], potential.at[:, pl.ds(c * LANES, LANES)], sem.at[1 + c]) for c in range(chunks)
    ]
    for c in leave:
        c.start()

    wide = picked.shape[0]

    def pick(g, carry):
        for u in range(16):
            i = g * 16 + u
            picked[pl.ds(i, 1), :] = flat[pl.ds(row_of[i], 1), :]
        return carry

    lax.fori_loop(0, wide // 16, pick, 0)
    deep = lax.broadcasted_iota(jnp.int32, (LANES, LANES), 0)
    for q in range(wide // LANES):
        turned = picked[q * LANES:(q + 1) * LANES, :].T
        chosen = jnp.where(deep == lane_of[q:q + 1, :], turned, 0.0)
        line = jnp.sum(chosen, axis=0, keepdims=True)
        values[:, :, q * LANES:(q + 1) * LANES] = jnp.broadcast_to(line[None], (values.shape[0], 1, LANES))
    for c in leave:
        c.wait()


def join(row_of, lane_of, block, change, own, got, devices):
    chunks, cells, _ = block.shape
    cy = (own[0].shape[1] - SUB) // 4
    cz = cells // cy
    nodes = row_of.shape[0]
    nx = chunks * LANES
    return pl.pallas_call(
        join_kernel,
        out_shape=(f32(cells, nx), f32(devices, 1, nodes)),
        in_specs=[SMEM, VMEM, ANY] + [VMEM] * 8,
        out_specs=(ANY, VMEM),
        scratch_shapes=[
            pltpu.VMEM((chunks, cells, LANES), jnp.float32),
            pltpu.VMEM((SLOTS, chunks, cy + 2 * SUB + 2 * PAD, LANES), jnp.float32),
            pltpu.VMEM((SLOTS, chunks, cz + 2 * SUB + 2 * PAD, LANES), jnp.float32),
            pltpu.VMEM((nodes, LANES), jnp.float32),
            pltpu.SemaphoreType.DMA((1 + chunks,)),
        ],
        compiler_params=pltpu.CompilerParams(vmem_limit_bytes=24 << 20),
        name="join",
    )(row_of, lane_of, block, change, *own, *got)


def window_kernel(table_ref, slot_ref, matrix_ref, keep_ref, send_ref, rows_ref):
    rows, columns = matrix_ref.shape
    owners, _, width = table_ref.shape
    parts = width // LANES
    count = owners * parts
    for q in range(parts):
        rows_ref[pl.ds(q, owners, stride=parts), :] = table_ref[:, 0, q * LANES:(q + 1) * LANES]
    turned = rows_ref[...].T
    high_part = turned.astype(jnp.bfloat16)
    low_part = (turned - high_part.astype(jnp.float32)).astype(jnp.bfloat16)
    halves = jnp.concatenate([high_part, low_part], axis=0)
    number = lax.broadcasted_iota(jnp.int32, (count, LANES), 0)
    deep = lax.broadcasted_iota(jnp.int32, (LANES, LANES), 0)
    blocks = rows // 16
    chunks = columns // LANES
    each = WINDOW_CHUNKS
    col = lax.axis_index("cols").astype(jnp.int32)
    first = col * chunks
    start = [pl.multiple_of(side * (rows // 2), SUB) for side in (col, 1 - col)]

    def part(i, accs):
        accs = list(accs)
        slots = [slot_ref[pl.ds(first + i * each + u, 1), :] for u in range(each)]
        hot = jnp.concatenate(
            [jnp.where(number == jnp.broadcast_to(s >> 7, (count, LANES)), 1.0, 0.0).astype(jnp.bfloat16) for s in slots],
            axis=1,
        )
        found = jnp.dot(halves, hot, preferred_element_type=jnp.float32)
        for u in range(each):
            both = found[:LANES, u * LANES:(u + 1) * LANES] + found[LANES:, u * LANES:(u + 1) * LANES]
            lane = jnp.broadcast_to(slots[u] & (LANES - 1), (LANES, LANES))
            line = jnp.sum(jnp.where(deep == lane, both, 0.0), axis=0, keepdims=True)
            value = jnp.broadcast_to(line, (SUB, LANES))
            at = i * (each * LANES) + u * LANES
            at = at if isinstance(i, int) else pl.multiple_of(at, LANES)
            for side in range(2):
                for b in range(blocks):
                    tile = matrix_ref[pl.ds(start[side] + SUB * b, SUB), pl.ds(at, LANES)]
                    accs[side * blocks + b] = accs[side * blocks + b] + tile * value
        return tuple(accs)

    zero = jnp.zeros((SUB, LANES), jnp.float32)
    accs = (zero,) * (2 * blocks)
    if chunks // each <= 4:
        for i in range(chunks // each):
            accs = part(i, accs)
    else:
        accs = lax.fori_loop(0, chunks // each, part, accs)
    for side, out in enumerate((keep_ref, send_ref)):
        tall = jnp.concatenate(list(accs[side * blocks:(side + 1) * blocks]) + [zero] * (16 - blocks), axis=0)
        out[...] = jnp.sum(tall.T, axis=0, keepdims=True)


WINDOW_CHUNKS = 24


def window_product(table, slots, matrix):
    rows, columns = matrix.shape
    assert columns % (WINDOW_CHUNKS * LANES) == 0 and rows % 16 == 0 and rows <= 2 * LANES
    out = f32(1, LANES)
    return pl.pallas_call(
        window_kernel,
        out_shape=(out, out),
        in_specs=[VMEM, VMEM, VMEM],
        out_specs=(VMEM, VMEM),
        scratch_shapes=[pltpu.VMEM((table.size // LANES, LANES), jnp.float32)],
        compiler_params=pltpu.CompilerParams(vmem_limit_bytes=32 << 20),
        name="window",
    )(table, slots, matrix)


def routes(n):
    def across(r):
        other = r + 1 if r % 2 else r - 1
        return other if 0 <= other < n else None

    near = [(r, r ^ 1) for r in range(n)]
    far, near_diag, far_diag = [], [], []
    for r in range(n):
        for c in range(2):
            other = across(r)
            far.append((r * 2 + c, r * 2 + 1 - c if other is None else other * 2 + c))
            near_diag.append((r * 2 + c, (r ^ 1) * 2 + 1 - c))
            far_diag.append((r * 2 + c, (r if other is None else other) * 2 + 1 - c))
    return near, far, near_diag, far_diag


def local(phi_start, source, owner_voxel, column_slot, layer_matrix):
    n = lax.axis_size("rows")
    assert lax.axis_size("cols") == 2 and n % 2 == 0
    devices = 2 * n
    cz, cy, nx = phi_start.shape
    near, far, near_diag, far_diag = routes(n)
    swap = [(0, 1), (1, 0)]

    pack_b, diag_b = far_face(phi_start, source)
    got_b = lax.ppermute(pack_b, BOTH, far)
    pack_a, pack_y, diag_a = near_face(diag_b, phi_start, source)
    got_db = lax.ppermute(diag_b, BOTH, far_diag)
    got_y = lax.ppermute(pack_y, "cols", swap)
    got_da = lax.ppermute(diag_a, BOTH, near_diag)
    got_a = lax.ppermute(pack_a, "rows", near)
    block, matrix = alone(phi_start, source, layer_matrix)
    x = owner_voxel % nx
    row_of = (x // LANES) * (cz * cy) + owner_voxel // nx
    lane_of = (x % LANES).reshape(-1, LANES)
    change = near_join(pack_a, got_a, got_da, got_y)
    potential, values = join(
        row_of, lane_of, block, change, (pack_b, pack_y), (got_a, got_b, got_y, got_da, got_db), devices
    )
    table = lax.all_to_all(values, BOTH, 0, 0, tiled=True)
    slots = column_slot.reshape(-1, LANES)
    keep, send = window_product(table, slots, matrix)
    received = lax.ppermute(send, "cols", swap)
    half = layer_matrix.shape[0] // 2
    return potential.reshape(cz, cy, nx), (keep + received)[0, :half]


def solution(mesh):
    return jax.shard_map(
        local,
        mesh=mesh,
        in_specs=(
            P("rows", "cols", None),
            P("rows", "cols", None),
            P(("rows", "cols")),
            P(),
            P("rows", "cols"),
        ),
        out_specs=(P("rows", "cols", None), P(("rows", "cols"))),
        check_vma=False,
    )
```

```python
import functools

import jax
import jax.numpy as jnp
from jax import lax
from jax.experimental import pallas as pl
from jax.experimental.pallas import tpu as pltpu
from jax.sharding import PartitionSpec as P

ITERS = 4
LANES = 128
SUB = 8
SIXTH = 1.0 / 6.0
LITTLE = pl.CostEstimate(flops=1, bytes_accessed=1, transcendentals=0)
FIRST_LIMIT = 58 << 20
BOTH = ("rows", "cols")
VMEM = pl.BlockSpec(memory_space=pltpu.VMEM)
SMEM = pl.BlockSpec(memory_space=pltpu.SMEM)
ANY = pl.BlockSpec(memory_space=pl.ANY)


def lanes_of(shape=(SUB, LANES)):
    return lax.broadcasted_iota(jnp.int32, shape, 1)


def subs_of(shape=(SUB, LANES)):
    return lax.broadcasted_iota(jnp.int32, shape, 0)


PAD = SUB


def around(ref, slot, rows):
    chunks = ref.shape[1]
    lane = lanes_of()
    zero = jnp.zeros((SUB, LANES), jnp.float32)
    out = []
    for b in range(rows // SUB):
        at = PAD + SUB * b
        here = [ref[slot, c, pl.ds(at, SUB), :] for c in range(chunks)]
        before = [pltpu.roll(t, 1, 1) for t in here]
        after = [pltpu.roll(t, LANES - 1, 1) for t in here]
        row = []
        for c in range(chunks):
            west = jnp.where(lane == 0, before[c - 1] if c else zero, before[c])
            east = jnp.where(lane == LANES - 1, after[c + 1] if c + 1 < chunks else zero, after[c])
            row.append((west + east) + (ref[slot, c, pl.ds(at - 1, SUB), :] + ref[slot, c, pl.ds(at + 1, SUB), :]))
        out.append(row)
    return out


def layer_of(ref, slot, rows):
    return [[ref[slot, c, pl.ds(PAD + SUB * b, SUB), :] for c in range(ref.shape[1])] for b in range(rows // SUB)]


def keep_layer(ref, slot, tiles):
    for b, row in enumerate(tiles):
        for c, tile in enumerate(row):
            ref[slot, c, pl.ds(PAD + SUB * b, SUB), :] = tile


def clear_pads(ref, slot, rows):
    zero = jnp.zeros((SUB, LANES), jnp.float32)
    for c in range(ref.shape[1]):
        ref[slot, c, 0:PAD, :] = zero
        ref[slot, c, PAD + rows:2 * PAD + rows, :] = zero


def load(ref, at, blocks):
    return [[ref[c, pl.ds(at + SUB * b, SUB), :] for c in range(ref.shape[0])] for b in range(blocks)]


def store(ref, at, tiles):
    for b, row in enumerate(tiles):
        for c, tile in enumerate(row):
            ref[c, pl.ds(at + SUB * b, SUB), :] = tile


def total(*terms):
    terms = [t for t in terms if t is not None]
    out = []
    for b in range(len(terms[0])):
        row = []
        for c in range(len(terms[0][0])):
            value = terms[0][b][c]
            for t in terms[1:]:
                value = value + t[b][c]
            row.append(value * SIXTH)
        out.append(row)
    return out


def spread(tile, i):
    return jnp.broadcast_to(tile[i:i + 1, :], (SUB, LANES))


def stack(rows):
    sub = subs_of()
    out = []
    for c in range(len(rows[0])):
        value = rows[0][c]
        for i in range(1, len(rows)):
            value = jnp.where(sub == i, rows[i][c], value)
        out.append(value)
    return out


def near_row(right, first, last, m):
    return [jnp.where(right, spread(f, m), spread(t, SUB - 1 - m)) for f, t in zip(first, last)]


def solve_face(first, source, p0, work, put, rows):
    first(0)
    put(0, layer_of(p0, 0, rows))
    for j in range(3):
        first(j + 1)
        back = layer_of(p0, j - 1, rows) if j else None
        keep_layer(work, j, total(source(j), around(p0, j, rows), layer_of(p0, j + 1, rows), back))
    one = [layer_of(work, j, rows) for j in range(3)]
    put(1, one[0])
    for j in range(2):
        keep_layer(work, 3 + j, total(source(j), around(work, j, rows), one[j + 1], one[j - 1] if j else None))
    two = [layer_of(work, 3 + j, rows) for j in range(2)]
    put(2, two[0])
    put(3, total(source(0), around(work, 3, rows), two[1]))


def fetch_face(phi, src, low, raw, sem):
    last = phi.shape[0] - 1
    copies = {}
    for i, j in ((0, 0), (0, 1), (1, 0), (0, 2), (1, 1), (0, 3), (1, 2)):
        z = jnp.where(low == 1, j, last - j)
        copies[i, j] = pltpu.make_async_copy((src if i else phi).at[z], raw.at[i, j], sem.at[i, j])
    return copies


def tiles_of(ref):
    rows, wide = ref.shape
    return [[ref[SUB * b:SUB * b + SUB, c * LANES:(c + 1) * LANES] for c in range(wide // LANES)] for b in range(rows // SUB)]


def send_face(right, first, source, p0, work, put, diag, cy):
    chunks = p0.shape[1]
    solve_face(first, source, p0, work, put, cy)

    def near(ref, slot, m):
        edges = [[ref[slot, c, pl.ds(at, SUB), :] for c in range(chunks)] for at in (PAD, PAD + cy - SUB)]
        return near_row(right, *edges, m)

    put(4, [near(p0, 1, 0)])
    store(diag, 0, [stack([
        near(p0, 0, 0), near(p0, 1, 0), near(p0, 2, 0), near(work, 0, 0), near(work, 1, 0),
        near(work, 3, 0), near(p0, 0, 1), near(p0, 0, 2),
    ])])
    store(diag, SUB, [near(work, 0, 1)])


def far_face_kernel(phi, src, pack, diag, raw, p0, work, sem):
    cy = phi.shape[1]
    odd, col, _ = whereabouts()
    copies = fetch_face(phi, src, 1 - odd, raw, sem)
    for c in copies.values():
        c.start()
    for i in range(4):
        clear_pads(p0, i, cy)
    for i in range(5):
        clear_pads(work, i, cy)
    def first(j):
        copies[0, j].wait()
        keep_layer(p0, j, tiles_of(raw.at[0, j]))

    def source(j, seen=set()):
        if j not in seen:
            seen.add(j)
            copies[1, j].wait()
        return tiles_of(raw.at[1, j])

    send_face(col == 1, first, source, p0, work, lambda k, tiles: store(pack, k * cy, tiles), diag, cy)


def f32(*shape):
    return jax.ShapeDtypeStruct(shape, jnp.float32)


def face_scratch(chunks, cy):
    tall = cy + 2 * PAD
    return [
        pltpu.VMEM((2, 4, cy, chunks * LANES), jnp.float32),
        pltpu.VMEM((4, chunks, tall, LANES), jnp.float32),
        pltpu.VMEM((5, chunks, tall, LANES), jnp.float32),
    ]


def whereabouts():
    n, r = lax.axis_size("rows"), lax.axis_index("rows").astype(jnp.int32)
    odd = lax.rem(r, 2)
    return odd, lax.axis_index("cols").astype(jnp.int32), jnp.where(odd == 1, r < n - 1, r > 0).astype(jnp.int32)


def far_face(phi, src):
    cz, cy, nx = phi.shape
    chunks = nx // LANES
    return pl.pallas_call(
        far_face_kernel,
        out_shape=(f32(chunks, 4 * cy + SUB, LANES), f32(chunks, 2 * SUB, LANES)),
        in_specs=[ANY, ANY],
        out_specs=(VMEM, VMEM),
        scratch_shapes=face_scratch(chunks, cy) + [pltpu.SemaphoreType.DMA((2, 4))],
        compiler_params=pltpu.CompilerParams(vmem_limit_bytes=FIRST_LIMIT),
        name="far_face",
    )(phi, src)


def near_face_kernel(after, phi, src, pack, pack_y, diag, p0, work, edge, edge_p, edge_w):
    cz, cy, nx = phi.shape
    chunks = nx // LANES
    odd, col, _ = whereabouts()
    right = col == 1
    for i in range(4):
        clear_pads(p0, i, cy)
        clear_pads(edge_p, i, cz)
    for i in range(5):
        clear_pads(work, i, cy)
        clear_pads(edge_w, i, cz)

    def layer(j):
        return jnp.where(odd == 1, j, cz - 1 - j)

    def first(j):
        keep_layer(p0, j, tiles_of(phi.at[layer(j)]))

    def put(k, tiles):
        if k < 4:
            store(pack, k * cy, tiles)
        else:
            for c, tile in enumerate(tiles[0]):
                pack[c, k * cy:k * cy + 1, :] = tile[:1, :]

    send_face(right, first, lambda j: tiles_of(src.at[layer(j)]), p0, work, put, diag, cy)
    at = pl.multiple_of(jnp.where(right, 0, cy - SUB), SUB)
    for i, whole in enumerate((phi, src)):
        for z in range(cz):
            for c in range(chunks):
                edge[i, c, z * SUB:(z + 1) * SUB, :] = whole[z, pl.ds(at, SUB), c * LANES:(c + 1) * LANES]
    flat = edge.reshape(2 * chunks * cz * SUB, LANES)

    def plane(i, c, m):
        row = jnp.where(right, m, SUB - 1 - m)
        return flat[pl.ds((i * chunks + c) * cz * SUB + row, cz, stride=SUB), :]

    def first_plane(m):
        for c in range(chunks):
            edge_p[m, c, PAD:PAD + cz, :] = plane(0, c, m)

    def source(m):
        whole = [plane(1, c, m) for c in range(chunks)]
        return [[w[SUB * b:SUB * b + SUB, :] for w in whole] for b in range(cz // SUB)]

    solve_face(first_plane, source, edge_p, edge_w, lambda k, tiles: store(pack_y, k * cz, tiles), cz)
    ends = [[edge_p[1, c, pl.ds(PAD + i, 1), :] for c in range(chunks)] for i in (0, cz - 1)]
    ends = [[jnp.broadcast_to(t, (SUB, LANES)) for t in row] for row in ends]
    own = [[jnp.where(odd == 1, a, b) for a, b in zip(*ends)], [jnp.where(odd == 1, b, a) for a, b in zip(*ends)]]
    store(pack_y, 4 * cz, [stack(own)])


def near_face(after, phi, src):
    cz, cy, nx = phi.shape
    chunks = nx // LANES
    tall = cz + 2 * PAD
    return pl.pallas_call(
        near_face_kernel,
        out_shape=(
            f32(chunks, 4 * cy + 1, LANES), f32(chunks, 4 * cz + SUB, LANES), f32(chunks, 2 * SUB, LANES),
        ),
        in_specs=[ANY, VMEM, VMEM],
        out_specs=(VMEM,) * 3,
        scratch_shapes=face_scratch(chunks, cy)[1:] + [
            pltpu.VMEM((2, chunks, cz * SUB, LANES), jnp.float32),
            pltpu.VMEM((4, chunks, tall, LANES), jnp.float32),
            pltpu.VMEM((5, chunks, tall, LANES), jnp.float32),
        ],
        compiler_params=pltpu.CompilerParams(vmem_limit_bytes=24 << 20),
        cost_estimate=LITTLE,
        name="near_face",
    )(after, phi, src)


def alone_kernel(phi, src, matrix, slots, out, matrix_out, hot, buf_a, buf_b, sem):
    cz, cy, nx = phi.shape
    blocks, chunks = cy // SUB, nx // LANES
    pieces = 4
    deep = matrix.shape[0] // pieces
    copies = [
        pltpu.make_async_copy(matrix.at[i * deep:(i + 1) * deep], matrix_out.at[i * deep:(i + 1) * deep], sem.at[i])
        for i in range(pieces)
    ]
    for c in copies:
        c.start()
    zero = [[jnp.zeros((SUB, LANES), jnp.float32)] * chunks] * blocks
    for ref in (buf_a, buf_b):
        for z in (0, cz + 1):
            keep_layer(ref, z, zero)

    def begin(z, carry):
        for ref in (buf_a, buf_b):
            clear_pads(ref, z + 1, cy)
        keep_layer(buf_a, z + 1, tiles_of(phi.at[z]))
        return carry

    lax.fori_loop(0, cz, begin, 0)
    for k in range(ITERS):
        here, there = (buf_a, buf_b) if k % 2 == 0 else (buf_b, buf_a)

        def layer(z, carry, here=here, there=there, last=k == ITERS - 1):
            value = total(tiles_of(src.at[z]), around(here, z + 1, cy), layer_of(here, z, cy), layer_of(here, z + 2, cy))
            if last:
                for c in range(chunks):
                    for b in range(blocks):
                        out[c, pl.ds(pl.multiple_of(z * cy, SUB) + SUB * b, SUB), :] = value[b][c]
            else:
                keep_layer(there, z + 1, value)
            return carry

        lax.fori_loop(0, cz, layer, 0, unroll=True)
    if hot.shape[0] == slots.shape[0]:
        first = lax.axis_index("cols").astype(jnp.int32) * (hot.shape[1] // LANES)
        number = lax.broadcasted_iota(jnp.int32, (hot.shape[0], LANES), 0)
        for u in range(hot.shape[1] // LANES):
            hot[:, u * LANES:(u + 1) * LANES] = one_hot(slots[pl.ds(first + u, 1), :], number)
    for c in copies:
        c.wait()


def alone(phi, src, matrix, slots):
    cz, cy, nx = phi.shape
    chunks = nx // LANES
    count, columns = slots.shape[0], matrix.shape[1]
    ahead = (count, columns) if count * columns <= 4 << 20 else (2 * SUB, LANES)
    return pl.pallas_call(
        alone_kernel,
        out_shape=(f32(chunks, cz * cy, LANES), f32(*matrix.shape), jax.ShapeDtypeStruct(ahead, jnp.bfloat16)),
        in_specs=[VMEM, VMEM, ANY, VMEM],
        out_specs=(VMEM,) * 3,
        scratch_shapes=[
            pltpu.VMEM((cz + 2, chunks, cy + 2 * PAD, LANES), jnp.float32),
            pltpu.VMEM((cz + 2, chunks, cy + 2 * PAD, LANES), jnp.float32),
            pltpu.SemaphoreType.DMA((4,)),
        ],
        compiler_params=pltpu.CompilerParams(vmem_limit_bytes=20 << 20),
        cost_estimate=LITTLE,
        name="alone",
    )(phi, src, matrix, slots)


def respond(rows, outer, inner, mask, work, finish):
    for slot in range(SLOTS):
        clear_pads(work, slot, rows)
    o0, i0, o0_2, i0_2, o1_2, i1_2, o0_3, i0_3, i1_3, i2_3 = range(SLOTS)

    def keep(slot, *terms):
        keep_layer(work, slot, mask(total(*terms)))

    def at(slot):
        return layer_of(work, slot, rows)

    def near(slot):
        return around(work, slot, rows)

    keep(o0, outer(0))
    keep(i0, inner(0))
    keep(o0_2, outer(1), near(o0), at(i0))
    keep(i0_2, inner(1), near(i0), at(o0))
    keep(o1_2, at(o0))
    keep(i1_2, at(i0))
    keep(o0_3, outer(2), near(o0_2), at(o1_2), at(i0_2))
    keep(i0_3, inner(2), near(i0_2), at(o0_2), at(i1_2))
    keep(i1_3, near(i1_2), at(i0_2))
    keep(i2_3, at(i1_2))
    finish(0, total(inner(3), near(i0_3), at(o0_3), at(i1_3)))
    finish(1, total(near(i1_3), at(i0_3), at(i2_3)))
    finish(2, total(near(i2_3), at(i1_3)))
    finish(3, total(at(i2_3)))


SLOTS = 10


def planes(refs, cy):
    each = 4 // len(refs)
    return lambda k: load(refs[k // each], k % each * cy, cy // SUB)


class Corner:
    def __init__(self, chunks):
        self.odd, col, has_far = whereabouts()
        self.right = col == 1
        self.has = (1.0, has_far.astype(jnp.float32))
        self.zero = [jnp.zeros((SUB, LANES), jnp.float32)] * chunks
        self.at_low = jnp.where(self.right, 1.0, 0.0)
        self.at_high = 1.0 - self.at_low

    def row(self, ref, at, i):
        return [spread(t, i) for t in load(ref, at, 1)[0]]

    def scale(self, tiles, factor):
        return [t * factor for t in tiles]

    def flank(self, rows, low):
        out, sub = self.zero, subs_of()
        for m, value in enumerate(rows):
            out = [jnp.where(sub == (SUB - 1 - m if low else m), v, o) for v, o in zip(value, out)]
        return out

    def near(self, ref, at, cy, m):
        return near_row(self.right, load(ref, at, 1)[0], load(ref, at + cy - SUB, 1)[0], m)

    def diag(self, ref, k, j=0, m=0):
        place = {(0, 0, 0): 0, (0, 1, 0): 1, (0, 2, 0): 2, (1, 0, 0): 3, (1, 1, 0): 4, (2, 0, 0): 5, (0, 0, 1): 6,
                 (0, 0, 2): 7, (1, 0, 1): 8}[(k, j, m)]
        return self.row(ref, place // SUB * SUB, place % SUB)

    def low_side(self, i):
        return self.odd if i == 0 else 1 - self.odd

    def add_layer(self, pot, i, j, cz, cy, tiles):
        start = pl.multiple_of(jnp.where(self.low_side(i) == 1, j, cz - 1 - j) * cy, SUB)
        for b, row in enumerate(tiles):
            for c, tile in enumerate(row):
                where = (c, pl.ds(start + SUB * b, SUB), slice(None))
                pot[where] = pot[where] + tile

    def interface(self, i, own, got, got_d, got_y, cz, cy, work, finish):
        low, blocks = self.low_side(i) == 1, cy // SUB

        def end_row(k):
            return [jnp.where(low, a, b) for a, b in zip(self.row(got_y, k * cz, 0), self.row(got_y, k * cz + cz - SUB, SUB - 1))]

        def driven(plane, rows):
            middle = [self.scale(t, self.has[i]) for t in plane]
            return ([self.scale(self.flank(rows, True), self.has[i] * self.at_low)] + middle
                    + [self.scale(self.flank(rows, False), self.has[i] * self.at_high)])

        def inner(k):
            return driven(got(k), [self.diag(got_d, k, m=m) for m in range(3 - k)])

        def outer(k):
            rows = [end_row(k)] if k < 2 else []
            if k == 0:
                rows.append(self.row(got_y, 4 * cz, i))
            return driven(own(k), rows)

        def mask(tiles):
            return [self.scale(tiles[0], self.at_low)] + tiles[1:-1] + [self.scale(tiles[-1], self.at_high)]

        respond(cy + 2 * SUB, outer, inner, mask, work, lambda j, tiles: finish(j, tiles[1:-1]))


def near_join_kernel(own, got, got_d, got_y, block, out, work):
    chunks, cells, _ = block.shape
    cy = (own.shape[1] - 1) // 4
    cz = cells // cy
    place = Corner(chunks)
    for z in range(cz):
        store(out, z * cy, load(block, z * cy, cy // SUB))
    place.interface(
        0, planes((own,), cy), planes((got,), cy), got_d, got_y, cz, cy, work,
        lambda j, tiles: place.add_layer(out, 0, j, cz, cy, tiles),
    )


def one_hot(slots, number):
    return jnp.where(number == jnp.broadcast_to(slots >> 7, number.shape), 1.0, 0.0).astype(jnp.bfloat16)


def near_join(own, got, got_d, got_y, block):
    chunks, tall, _ = own.shape
    cy = (tall - 1) // 4
    return pl.pallas_call(
        near_join_kernel,
        out_shape=f32(*block.shape),
        in_specs=[VMEM] * 5,
        out_specs=VMEM,
        scratch_shapes=[pltpu.VMEM((SLOTS, chunks, cy + 2 * SUB + 2 * PAD, LANES), jnp.float32)],
        compiler_params=pltpu.CompilerParams(vmem_limit_bytes=24 << 20),
        name="near_join",
    )(own, got, got_d, got_y, block)


def join_kernel(
    row_of, lane_of, block, own_b, own_y, got_a, got_b, got_y, got_da, got_db,
    potential, values, pot, layers, columns, picked, sem,
):
    chunks, cells, _ = pot.shape
    cy = (own_b.shape[1] - SUB) // 4
    cz = cells // cy
    blocks = cy // SUB
    place = Corner(chunks)
    odd, right, has = place.odd, place.right, place.has
    sub = subs_of()
    for z in range(cz):
        store(pot, z * cy, load(block, z * cy, blocks))

    def finish(j, tiles):
        place.add_layer(pot, 1, j, cz, cy, tiles)

    place.interface(1, planes((own_b,), cy), planes((got_b,), cy), got_db, got_y, cz, cy, layers, finish)

    low_has = jnp.where(odd == 1, has[0], has[1])
    high_has = jnp.where(odd == 1, has[1], has[0])

    def either(a, b):
        return [jnp.where(odd == 1, x, y) for x, y in zip(a, b)], [jnp.where(odd == 1, y, x) for x, y in zip(a, b)]

    def along(plane, pairs):
        low = place.scale(place.flank([p[0] for p in pairs], True), low_has)
        high = place.scale(place.flank([p[1] for p in pairs], False), high_has)
        return [low] + plane + [high]

    def inner_y(k):
        pairs = [either(place.diag(got_da, k, j=j), place.diag(got_db, k, j=j)) for j in range(3 - k)]
        return along(load(got_y, k * cz, cz // SUB), pairs)

    def outer_y(k):
        pairs = [either(place.near(got_a, k * cy, cy, 0), place.near(got_b, k * cy, cy, 0))] if k < 2 else []
        if k == 0:
            pairs.append(either([jnp.broadcast_to(got_a[c, 4 * cy:4 * cy + 1, :], (SUB, LANES)) for c in range(chunks)], place.row(got_b, 4 * cy, 0)))
        return along(load(own_y, k * cz, cz // SUB), pairs)

    def mask_y(tiles):
        return [place.scale(tiles[0], low_has)] + tiles[1:-1] + [place.scale(tiles[-1], high_has)]

    flat = pot.reshape(chunks * cells, LANES)

    def finish_y(j, tiles):
        row = jnp.where(right, j, cy - 1 - j)
        for c in range(chunks):
            for half in range(cz // SUB):
                where = (pl.ds(c * cells + half * SUB * cy + row, SUB, stride=cy), slice(None))
                flat[where] = flat[where] + tiles[half + 1][c]

    respond(cz + 2 * SUB, outer_y, inner_y, mask_y, columns, finish_y)

    leave = [
        pltpu.make_async_copy(pot.at[c], potential.at[:, pl.ds(c * LANES, LANES)], sem.at[c]) for c in range(chunks)
    ]
    for c in leave:
        c.start()

    wide = picked.shape[0]

    def pick(g, carry):
        for u in range(16):
            i = g * 16 + u
            picked[pl.ds(i, 1), :] = flat[pl.ds(row_of[i], 1), :]
        return carry

    lax.fori_loop(0, wide // 16, pick, 0)
    deep = lax.broadcasted_iota(jnp.int32, (LANES, LANES), 0)
    for q in range(wide // LANES):
        turned = picked[q * LANES:(q + 1) * LANES, :].T
        chosen = jnp.where(deep == lane_of[q:q + 1, :], turned, 0.0)
        line = jnp.sum(chosen, axis=0, keepdims=True)
        values[:, :, q * LANES:(q + 1) * LANES] = jnp.broadcast_to(line[None], (values.shape[0], 1, LANES))
    for c in leave:
        c.wait()


def join(row_of, lane_of, block, own, got, devices):
    chunks, cells, _ = block.shape
    cy = (own[0].shape[1] - SUB) // 4
    cz = cells // cy
    nodes = row_of.shape[0]
    return pl.pallas_call(
        join_kernel,
        out_shape=(f32(cells, chunks * LANES), f32(devices, 1, nodes)),
        in_specs=[SMEM, VMEM, VMEM] + [VMEM] * 7,
        out_specs=(ANY, VMEM),
        scratch_shapes=[
            pltpu.VMEM((chunks, cells, LANES), jnp.float32),
            pltpu.VMEM((SLOTS, chunks, cy + 2 * SUB + 2 * PAD, LANES), jnp.float32),
            pltpu.VMEM((SLOTS, chunks, cz + 2 * SUB + 2 * PAD, LANES), jnp.float32),
            pltpu.VMEM((nodes, LANES), jnp.float32),
            pltpu.SemaphoreType.DMA((chunks,)),
        ],
        compiler_params=pltpu.CompilerParams(vmem_limit_bytes=24 << 20),
        name="join",
    )(row_of, lane_of, block, *own, *got)


def window_kernel(table_ref, slot_ref, matrix_ref, hot_ref, keep_ref, send_ref, rows_ref):
    rows, columns = matrix_ref.shape
    owners, _, width = table_ref.shape
    parts = width // LANES
    count = owners * parts
    for q in range(parts):
        rows_ref[pl.ds(q, owners, stride=parts), :] = table_ref[:, 0, q * LANES:(q + 1) * LANES]
    turned = rows_ref[...].T
    high_part = turned.astype(jnp.bfloat16)
    low_part = (turned - high_part.astype(jnp.float32)).astype(jnp.bfloat16)
    halves = jnp.concatenate([high_part, low_part], axis=0)
    number = lax.broadcasted_iota(jnp.int32, (count, LANES), 0)
    deep = lax.broadcasted_iota(jnp.int32, (LANES, LANES), 0)
    blocks = rows // 16
    chunks = columns // LANES
    each = WINDOW_CHUNKS
    col = lax.axis_index("cols").astype(jnp.int32)
    first = col * chunks
    start = [pl.multiple_of(side * (rows // 2), SUB) for side in (col, 1 - col)]

    def part(i, accs):
        accs = list(accs)
        slots = [slot_ref[pl.ds(first + i * each + u, 1), :] for u in range(each)]
        at = i * (each * LANES)
        if hot_ref.shape[0] == count:
            hot = hot_ref[:, pl.ds(at if isinstance(i, int) else pl.multiple_of(at, LANES), each * LANES)]
        else:
            hot = jnp.concatenate([one_hot(s, number) for s in slots], axis=1)
        found = jnp.dot(halves, hot, preferred_element_type=jnp.float32)
        for u in range(each):
            both = found[:LANES, u * LANES:(u + 1) * LANES] + found[LANES:, u * LANES:(u + 1) * LANES]
            lane = jnp.broadcast_to(slots[u] & (LANES - 1), (LANES, LANES))
            line = jnp.sum(jnp.where(deep == lane, both, 0.0), axis=0, keepdims=True)
            value = jnp.broadcast_to(line, (SUB, LANES))
            at = i * (each * LANES) + u * LANES
            at = at if isinstance(i, int) else pl.multiple_of(at, LANES)
            for side in range(2):
                for b in range(blocks):
                    tile = matrix_ref[pl.ds(start[side] + SUB * b, SUB), pl.ds(at, LANES)]
                    accs[side * blocks + b] = accs[side * blocks + b] + tile * value
        return tuple(accs)

    zero = jnp.zeros((SUB, LANES), jnp.float32)
    accs = (zero,) * (2 * blocks)
    if chunks // each <= 4:
        for i in range(chunks // each):
            accs = part(i, accs)
    else:
        accs = lax.fori_loop(0, chunks // each, part, accs)
    for side, out in enumerate((keep_ref, send_ref)):
        tall = jnp.concatenate(list(accs[side * blocks:(side + 1) * blocks]) + [zero] * (16 - blocks), axis=0)
        out[...] = jnp.sum(tall.T, axis=0, keepdims=True)


WINDOW_CHUNKS = 24


def window_product(table, slots, matrix, hot):
    rows, columns = matrix.shape
    assert columns % (WINDOW_CHUNKS * LANES) == 0 and rows % 16 == 0 and rows <= 2 * LANES
    out = f32(1, LANES)
    return pl.pallas_call(
        window_kernel,
        out_shape=(out, out),
        in_specs=[VMEM] * 4,
        out_specs=(VMEM, VMEM),
        scratch_shapes=[pltpu.VMEM((table.size // LANES, LANES), jnp.float32)],
        compiler_params=pltpu.CompilerParams(vmem_limit_bytes=32 << 20),
        name="window",
    )(table, slots, matrix, hot)


def routes(n):
    def across(r):
        other = r + 1 if r % 2 else r - 1
        return other if 0 <= other < n else None

    near = [(r, r ^ 1) for r in range(n)]
    far, near_diag, far_diag = [], [], []
    for r in range(n):
        for c in range(2):
            other = across(r)
            far.append((r * 2 + c, r * 2 + 1 - c if other is None else other * 2 + c))
            near_diag.append((r * 2 + c, (r ^ 1) * 2 + 1 - c))
            far_diag.append((r * 2 + c, (r if other is None else other) * 2 + 1 - c))
    return near, far, near_diag, far_diag


def local(phi_start, source, owner_voxel, column_slot, layer_matrix):
    n = lax.axis_size("rows")
    assert lax.axis_size("cols") == 2 and n % 2 == 0
    devices = 2 * n
    cz, cy, nx = phi_start.shape
    near, far, near_diag, far_diag = routes(n)
    swap = [(0, 1), (1, 0)]

    pack_b, diag_b = far_face(phi_start, source)
    got_b = lax.ppermute(pack_b, BOTH, far)
    pack_a, pack_y, diag_a = near_face(diag_b, phi_start, source)
    got_db = lax.ppermute(diag_b, BOTH, far_diag)
    got_y = lax.ppermute(pack_y, "cols", swap)
    got_da = lax.ppermute(diag_a, BOTH, near_diag)
    got_a = lax.ppermute(pack_a, "rows", near)
    slots = column_slot.reshape(-1, LANES)
    block, matrix, hot = alone(phi_start, source, layer_matrix, slots)
    x = owner_voxel % nx
    row_of = (x // LANES) * (cz * cy) + owner_voxel // nx
    lane_of = (x % LANES).reshape(-1, LANES)
    block = near_join(pack_a, got_a, got_da, got_y, block)
    potential, values = join(
        row_of, lane_of, block, (pack_b, pack_y), (got_a, got_b, got_y, got_da, got_db), devices
    )
    table = lax.all_to_all(values, BOTH, 0, 0, tiled=True)
    keep, send = window_product(table, slots, matrix, hot)
    received = lax.ppermute(send, "cols", swap)
    half = layer_matrix.shape[0] // 2
    return potential.reshape(cz, cy, nx), (keep + received)[0, :half]


def solution(mesh):
    return jax.shard_map(
        local,
        mesh=mesh,
        in_specs=(
            P("rows", "cols", None),
            P("rows", "cols", None),
            P(("rows", "cols")),
            P(),
            P("rows", "cols"),
        ),
        out_specs=(P("rows", "cols", None), P(("rows", "cols"))),
        check_vma=False,
    )
```

```python
import functools

import jax
import jax.numpy as jnp
from jax import lax
from jax.experimental import pallas as pl
from jax.experimental.pallas import tpu as pltpu
from jax.sharding import PartitionSpec as P

ITERS = 4
LANES = 128
SUB = 8
SIXTH = 1.0 / 6.0
LITTLE = pl.CostEstimate(flops=1, bytes_accessed=1, transcendentals=0)
FIRST_LIMIT = 58 << 20
BOTH = ("rows", "cols")
VMEM = pl.BlockSpec(memory_space=pltpu.VMEM)
SMEM = pl.BlockSpec(memory_space=pltpu.SMEM)
ANY = pl.BlockSpec(memory_space=pl.ANY)


def lanes_of(shape=(SUB, LANES)):
    return lax.broadcasted_iota(jnp.int32, shape, 1)


def subs_of(shape=(SUB, LANES)):
    return lax.broadcasted_iota(jnp.int32, shape, 0)


PAD = SUB


def around(ref, slot, rows):
    chunks = ref.shape[1]
    lane = lanes_of()
    zero = jnp.zeros((SUB, LANES), jnp.float32)
    out = []
    for b in range(rows // SUB):
        at = PAD + SUB * b
        here = [ref[slot, c, pl.ds(at, SUB), :] for c in range(chunks)]
        before = [pltpu.roll(t, 1, 1) for t in here]
        after = [pltpu.roll(t, LANES - 1, 1) for t in here]
        row = []
        for c in range(chunks):
            west = jnp.where(lane == 0, before[c - 1] if c else zero, before[c])
            east = jnp.where(lane == LANES - 1, after[c + 1] if c + 1 < chunks else zero, after[c])
            row.append((west + east) + (ref[slot, c, pl.ds(at - 1, SUB), :] + ref[slot, c, pl.ds(at + 1, SUB), :]))
        out.append(row)
    return out


def layer_of(ref, slot, rows):
    return [[ref[slot, c, pl.ds(PAD + SUB * b, SUB), :] for c in range(ref.shape[1])] for b in range(rows // SUB)]


def keep_layer(ref, slot, tiles):
    for b, row in enumerate(tiles):
        for c, tile in enumerate(row):
            ref[slot, c, pl.ds(PAD + SUB * b, SUB), :] = tile


def clear_pads(ref, slot, rows):
    zero = jnp.zeros((SUB, LANES), jnp.float32)
    for c in range(ref.shape[1]):
        ref[slot, c, 0:PAD, :] = zero
        ref[slot, c, PAD + rows:2 * PAD + rows, :] = zero


def load(ref, at, blocks):
    return [[ref[c, pl.ds(at + SUB * b, SUB), :] for c in range(ref.shape[0])] for b in range(blocks)]


def store(ref, at, tiles):
    for b, row in enumerate(tiles):
        for c, tile in enumerate(row):
            ref[c, pl.ds(at + SUB * b, SUB), :] = tile


def total(*terms):
    terms = [t for t in terms if t is not None]
    out = []
    for b in range(len(terms[0])):
        row = []
        for c in range(len(terms[0][0])):
            value = terms[0][b][c]
            for t in terms[1:]:
                value = value + t[b][c]
            row.append(value * SIXTH)
        out.append(row)
    return out


def spread(tile, i):
    return jnp.broadcast_to(tile[i:i + 1, :], (SUB, LANES))


def stack(rows):
    sub = subs_of()
    out = []
    for c in range(len(rows[0])):
        value = rows[0][c]
        for i in range(1, len(rows)):
            value = jnp.where(sub == i, rows[i][c], value)
        out.append(value)
    return out


def near_row(right, first, last, m):
    return [jnp.where(right, spread(f, m), spread(t, SUB - 1 - m)) for f, t in zip(first, last)]


def solve_face(first, source, p0, work, put, rows):
    first(0)
    put(0, layer_of(p0, 0, rows))
    for j in range(3):
        first(j + 1)
        back = layer_of(p0, j - 1, rows) if j else None
        keep_layer(work, j, total(source(j), around(p0, j, rows), layer_of(p0, j + 1, rows), back))
    one = [layer_of(work, j, rows) for j in range(3)]
    put(1, one[0])
    for j in range(2):
        keep_layer(work, 3 + j, total(source(j), around(work, j, rows), one[j + 1], one[j - 1] if j else None))
    two = [layer_of(work, 3 + j, rows) for j in range(2)]
    put(2, two[0])
    put(3, total(source(0), around(work, 3, rows), two[1]))


def fetch_face(phi, src, low, raw, sem):
    last = phi.shape[0] - 1
    copies = {}
    for i, j in ((0, 0), (0, 1), (1, 0), (0, 2), (1, 1), (0, 3), (1, 2)):
        z = jnp.where(low == 1, j, last - j)
        copies[i, j] = pltpu.make_async_copy((src if i else phi).at[z], raw.at[i, j], sem.at[i, j])
    return copies


def tiles_of(ref):
    rows, wide = ref.shape
    return [[ref[SUB * b:SUB * b + SUB, c * LANES:(c + 1) * LANES] for c in range(wide // LANES)] for b in range(rows // SUB)]


def send_face(right, first, source, p0, work, put, diag, cy):
    chunks = p0.shape[1]
    solve_face(first, source, p0, work, put, cy)

    def near(ref, slot, m):
        edges = [[ref[slot, c, pl.ds(at, SUB), :] for c in range(chunks)] for at in (PAD, PAD + cy - SUB)]
        return near_row(right, *edges, m)

    put(4, [near(p0, 1, 0)])
    store(diag, 0, [stack([
        near(p0, 0, 0), near(p0, 1, 0), near(p0, 2, 0), near(work, 0, 0), near(work, 1, 0),
        near(work, 3, 0), near(p0, 0, 1), near(p0, 0, 2),
    ])])
    store(diag, SUB, [near(work, 0, 1)])


def far_face_kernel(phi, src, pack, diag, raw, p0, work, sem):
    cy = phi.shape[1]
    odd, col, _ = whereabouts()
    copies = fetch_face(phi, src, 1 - odd, raw, sem)
    for c in copies.values():
        c.start()
    for i in range(4):
        clear_pads(p0, i, cy)
    for i in range(5):
        clear_pads(work, i, cy)
    def first(j):
        copies[0, j].wait()
        keep_layer(p0, j, tiles_of(raw.at[0, j]))

    def source(j, seen=set()):
        if j not in seen:
            seen.add(j)
            copies[1, j].wait()
        return tiles_of(raw.at[1, j])

    send_face(col == 1, first, source, p0, work, lambda k, tiles: store(pack, k * cy, tiles), diag, cy)


def f32(*shape):
    return jax.ShapeDtypeStruct(shape, jnp.float32)


def face_scratch(chunks, cy):
    tall = cy + 2 * PAD
    return [
        pltpu.VMEM((2, 4, cy, chunks * LANES), jnp.float32),
        pltpu.VMEM((4, chunks, tall, LANES), jnp.float32),
        pltpu.VMEM((5, chunks, tall, LANES), jnp.float32),
    ]


def whereabouts():
    n, r = lax.axis_size("rows"), lax.axis_index("rows").astype(jnp.int32)
    odd = lax.rem(r, 2)
    return odd, lax.axis_index("cols").astype(jnp.int32), jnp.where(odd == 1, r < n - 1, r > 0).astype(jnp.int32)


def far_face(phi, src):
    cz, cy, nx = phi.shape
    chunks = nx // LANES
    return pl.pallas_call(
        far_face_kernel,
        out_shape=(f32(chunks, 4 * cy + SUB, LANES), f32(chunks, 2 * SUB, LANES)),
        in_specs=[ANY, ANY],
        out_specs=(VMEM, VMEM),
        scratch_shapes=face_scratch(chunks, cy) + [pltpu.SemaphoreType.DMA((2, 4))],
        compiler_params=pltpu.CompilerParams(vmem_limit_bytes=FIRST_LIMIT),
        name="far_face",
    )(phi, src)


def near_face_kernel(after, phi, src, pack, pack_y, diag, p0, work, edge, edge_p, edge_w):
    cz, cy, nx = phi.shape
    chunks = nx // LANES
    odd, col, _ = whereabouts()
    right = col == 1
    for i in range(4):
        clear_pads(p0, i, cy)
        clear_pads(edge_p, i, cz)
    for i in range(5):
        clear_pads(work, i, cy)
        clear_pads(edge_w, i, cz)

    def layer(j):
        return jnp.where(odd == 1, j, cz - 1 - j)

    def first(j):
        keep_layer(p0, j, tiles_of(phi.at[layer(j)]))

    def put(k, tiles):
        if k < 4:
            store(pack, k * cy, tiles)
        else:
            for c, tile in enumerate(tiles[0]):
                pack[c, k * cy:k * cy + 1, :] = tile[:1, :]

    send_face(right, first, lambda j: tiles_of(src.at[layer(j)]), p0, work, put, diag, cy)
    at = pl.multiple_of(jnp.where(right, 0, cy - SUB), SUB)
    for i, whole in enumerate((phi, src)):
        for z in range(cz):
            for c in range(chunks):
                edge[i, c, z * SUB:(z + 1) * SUB, :] = whole[z, pl.ds(at, SUB), c * LANES:(c + 1) * LANES]
    flat = edge.reshape(2 * chunks * cz * SUB, LANES)

    def plane(i, c, m):
        row = jnp.where(right, m, SUB - 1 - m)
        return flat[pl.ds((i * chunks + c) * cz * SUB + row, cz, stride=SUB), :]

    def first_plane(m):
        for c in range(chunks):
            edge_p[m, c, PAD:PAD + cz, :] = plane(0, c, m)

    def source(m):
        whole = [plane(1, c, m) for c in range(chunks)]
        return [[w[SUB * b:SUB * b + SUB, :] for w in whole] for b in range(cz // SUB)]

    solve_face(first_plane, source, edge_p, edge_w, lambda k, tiles: store(pack_y, k * cz, tiles), cz)
    ends = [[edge_p[1, c, pl.ds(PAD + i, 1), :] for c in range(chunks)] for i in (0, cz - 1)]
    ends = [[jnp.broadcast_to(t, (SUB, LANES)) for t in row] for row in ends]
    own = [[jnp.where(odd == 1, a, b) for a, b in zip(*ends)], [jnp.where(odd == 1, b, a) for a, b in zip(*ends)]]
    store(pack_y, 4 * cz, [stack(own)])


def near_face(after, phi, src):
    cz, cy, nx = phi.shape
    chunks = nx // LANES
    tall = cz + 2 * PAD
    return pl.pallas_call(
        near_face_kernel,
        out_shape=(
            f32(chunks, 4 * cy + 1, LANES), f32(chunks, 4 * cz + SUB, LANES), f32(chunks, 2 * SUB, LANES),
        ),
        in_specs=[ANY, VMEM, VMEM],
        out_specs=(VMEM,) * 3,
        scratch_shapes=face_scratch(chunks, cy)[1:] + [
            pltpu.VMEM((2, chunks, cz * SUB, LANES), jnp.float32),
            pltpu.VMEM((4, chunks, tall, LANES), jnp.float32),
            pltpu.VMEM((5, chunks, tall, LANES), jnp.float32),
        ],
        compiler_params=pltpu.CompilerParams(vmem_limit_bytes=24 << 20),
        cost_estimate=LITTLE,
        name="near_face",
    )(after, phi, src)


def alone_kernel(phi, src, matrix, slots, out, matrix_out, hot, buf_a, buf_b, sem):
    cz, cy, nx = phi.shape
    blocks, chunks = cy // SUB, nx // LANES
    pieces = 4
    deep = matrix.shape[0] // pieces
    copies = [
        pltpu.make_async_copy(matrix.at[i * deep:(i + 1) * deep], matrix_out.at[i * deep:(i + 1) * deep], sem.at[i])
        for i in range(pieces)
    ]
    for c in copies:
        c.start()
    zero = [[jnp.zeros((SUB, LANES), jnp.float32)] * chunks] * blocks
    for ref in (buf_a, buf_b):
        for z in (0, cz + 1):
            keep_layer(ref, z, zero)

    def begin(z, carry):
        for ref in (buf_a, buf_b):
            clear_pads(ref, z + 1, cy)
        keep_layer(buf_a, z + 1, tiles_of(phi.at[z]))
        return carry

    lax.fori_loop(0, cz, begin, 0)
    for k in range(ITERS):
        here, there = (buf_a, buf_b) if k % 2 == 0 else (buf_b, buf_a)

        def layer(z, carry, here=here, there=there, last=k == ITERS - 1):
            value = total(tiles_of(src.at[z]), around(here, z + 1, cy), layer_of(here, z, cy), layer_of(here, z + 2, cy))
            if last:
                for c in range(chunks):
                    for b in range(blocks):
                        out[c, pl.ds(pl.multiple_of(z * cy, SUB) + SUB * b, SUB), :] = value[b][c]
            else:
                keep_layer(there, z + 1, value)
            return carry

        lax.fori_loop(0, cz, layer, 0, unroll=True)
    if hot.shape[0] == slots.shape[0]:
        first = lax.axis_index("cols").astype(jnp.int32) * (hot.shape[1] // LANES)
        number = lax.broadcasted_iota(jnp.int32, (hot.shape[0], LANES), 0)
        for u in range(hot.shape[1] // LANES):
            hot[:, u * LANES:(u + 1) * LANES] = one_hot(slots[pl.ds(first + u, 1), :], number)
    for c in copies:
        c.wait()


def alone(phi, src, matrix, slots):
    cz, cy, nx = phi.shape
    chunks = nx // LANES
    count, columns = slots.shape[0], matrix.shape[1]
    ahead = (count, columns) if count * columns <= 4 << 20 else (2 * SUB, LANES)
    return pl.pallas_call(
        alone_kernel,
        out_shape=(f32(chunks, cz * cy, LANES), f32(*matrix.shape), jax.ShapeDtypeStruct(ahead, jnp.bfloat16)),
        in_specs=[VMEM, VMEM, ANY, VMEM],
        out_specs=(VMEM,) * 3,
        scratch_shapes=[
            pltpu.VMEM((cz + 2, chunks, cy + 2 * PAD, LANES), jnp.float32),
            pltpu.VMEM((cz + 2, chunks, cy + 2 * PAD, LANES), jnp.float32),
            pltpu.SemaphoreType.DMA((4,)),
        ],
        compiler_params=pltpu.CompilerParams(vmem_limit_bytes=20 << 20),
        cost_estimate=LITTLE,
        name="alone",
    )(phi, src, matrix, slots)


def respond(rows, outer, inner, mask, work, finish):
    for slot in range(SLOTS):
        clear_pads(work, slot, rows)
    o0, i0, o0_2, i0_2, o1_2, i1_2, o0_3, i0_3, i1_3, i2_3 = range(SLOTS)

    def keep(slot, *terms):
        keep_layer(work, slot, mask(total(*terms)))

    def at(slot):
        return layer_of(work, slot, rows)

    def near(slot):
        return around(work, slot, rows)

    keep(o0, outer(0))
    keep(i0, inner(0))
    keep(o0_2, outer(1), near(o0), at(i0))
    keep(i0_2, inner(1), near(i0), at(o0))
    keep(o1_2, at(o0))
    keep(i1_2, at(i0))
    keep(o0_3, outer(2), near(o0_2), at(o1_2), at(i0_2))
    keep(i0_3, inner(2), near(i0_2), at(o0_2), at(i1_2))
    keep(i1_3, near(i1_2), at(i0_2))
    keep(i2_3, at(i1_2))
    finish(0, total(inner(3), near(i0_3), at(o0_3), at(i1_3)))
    finish(1, total(near(i1_3), at(i0_3), at(i2_3)))
    finish(2, total(near(i2_3), at(i1_3)))
    finish(3, total(at(i2_3)))


SLOTS = 10


def planes(refs, cy):
    each = 4 // len(refs)
    return lambda k: load(refs[k // each], k % each * cy, cy // SUB)


class Corner:
    def __init__(self, chunks):
        self.odd, col, has_far = whereabouts()
        self.right = col == 1
        self.has = (1.0, has_far.astype(jnp.float32))
        self.zero = [jnp.zeros((SUB, LANES), jnp.float32)] * chunks
        self.at_low = jnp.where(self.right, 1.0, 0.0)
        self.at_high = 1.0 - self.at_low

    def row(self, ref, at, i):
        return [spread(t, i) for t in load(ref, at, 1)[0]]

    def scale(self, tiles, factor):
        return [t * factor for t in tiles]

    def flank(self, rows, low):
        out, sub = self.zero, subs_of()
        for m, value in enumerate(rows):
            out = [jnp.where(sub == (SUB - 1 - m if low else m), v, o) for v, o in zip(value, out)]
        return out

    def near(self, ref, at, cy, m):
        return near_row(self.right, load(ref, at, 1)[0], load(ref, at + cy - SUB, 1)[0], m)

    def diag(self, ref, k, j=0, m=0):
        place = {(0, 0, 0): 0, (0, 1, 0): 1, (0, 2, 0): 2, (1, 0, 0): 3, (1, 1, 0): 4, (2, 0, 0): 5, (0, 0, 1): 6,
                 (0, 0, 2): 7, (1, 0, 1): 8}[(k, j, m)]
        return self.row(ref, place // SUB * SUB, place % SUB)

    def low_side(self, i):
        return self.odd if i == 0 else 1 - self.odd

    def add_layer(self, pot, i, j, cz, cy, tiles):
        start = pl.multiple_of(jnp.where(self.low_side(i) == 1, j, cz - 1 - j) * cy, SUB)
        for b, row in enumerate(tiles):
            for c, tile in enumerate(row):
                where = (c, pl.ds(start + SUB * b, SUB), slice(None))
                pot[where] = pot[where] + tile

    def interface(self, i, own, got, got_d, got_y, cz, cy, work, finish):
        low, blocks = self.low_side(i) == 1, cy // SUB

        def end_row(k):
            return [jnp.where(low, a, b) for a, b in zip(self.row(got_y, k * cz, 0), self.row(got_y, k * cz + cz - SUB, SUB - 1))]

        def driven(plane, rows):
            middle = [self.scale(t, self.has[i]) for t in plane]
            return ([self.scale(self.flank(rows, True), self.has[i] * self.at_low)] + middle
                    + [self.scale(self.flank(rows, False), self.has[i] * self.at_high)])

        def inner(k):
            return driven(got(k), [self.diag(got_d, k, m=m) for m in range(3 - k)])

        def outer(k):
            rows = [end_row(k)] if k < 2 else []
            if k == 0:
                rows.append(self.row(got_y, 4 * cz, i))
            return driven(own(k), rows)

        def mask(tiles):
            return [self.scale(tiles[0], self.at_low)] + tiles[1:-1] + [self.scale(tiles[-1], self.at_high)]

        respond(cy + 2 * SUB, outer, inner, mask, work, lambda j, tiles: finish(j, tiles[1:-1]))


def near_join_kernel(own, got, got_d, got_y, block, out, work):
    chunks, cells, _ = block.shape
    cy = (own.shape[1] - 1) // 4
    cz = cells // cy
    place = Corner(chunks)
    for z in range(cz):
        store(out, z * cy, load(block, z * cy, cy // SUB))
    place.interface(
        0, planes((own,), cy), planes((got,), cy), got_d, got_y, cz, cy, work,
        lambda j, tiles: place.add_layer(out, 0, j, cz, cy, tiles),
    )


def one_hot(slots, number):
    return jnp.where(number == jnp.broadcast_to(slots >> 7, number.shape), 1.0, 0.0).astype(jnp.bfloat16)


def near_join(own, got, got_d, got_y, block):
    chunks, tall, _ = own.shape
    cy = (tall - 1) // 4
    return pl.pallas_call(
        near_join_kernel,
        out_shape=f32(*block.shape),
        in_specs=[VMEM] * 5,
        out_specs=VMEM,
        scratch_shapes=[pltpu.VMEM((SLOTS, chunks, cy + 2 * SUB + 2 * PAD, LANES), jnp.float32)],
        compiler_params=pltpu.CompilerParams(vmem_limit_bytes=24 << 20),
        name="near_join",
    )(own, got, got_d, got_y, block)


def join_kernel(
    row_of, lane_of, block, own_b, own_y, got_a, got_b, got_y, got_da, got_db,
    potential, values, pot, layers, columns, picked, sem,
):
    chunks, cells, _ = pot.shape
    cy = (own_b.shape[1] - SUB) // 4
    cz = cells // cy
    blocks = cy // SUB
    place = Corner(chunks)
    odd, right, has = place.odd, place.right, place.has
    deep = 4
    low_b = place.low_side(1) == 1
    rest, reach = jnp.where(low_b, deep, 0), jnp.where(low_b, 0, cz - deep)
    edge = pl.multiple_of(jnp.where(right, 0, cy - SUB), SUB)
    inner_rows = pl.multiple_of(jnp.where(right, SUB, 0), SUB)

    def leaving(ref, z, layers_out, y, rows, i):
        whole = ref.reshape(chunks, cz, cy, LANES)
        return [
            pltpu.make_async_copy(
                whole.at[c, pl.ds(z, layers_out), pl.ds(y, rows), :],
                potential.at[pl.ds(z, layers_out), pl.ds(y, rows), pl.ds(c * LANES, LANES)],
                sem.at[i, c],
            )
            for c in range(chunks)
        ]

    leave = leaving(block, rest, cz - deep, inner_rows, cy - SUB, 0)
    for c in leave:
        c.start()
    for z in range(cz):
        store(pot, z * cy, load(block, z * cy, blocks))

    def finish(j, tiles):
        place.add_layer(pot, 1, j, cz, cy, tiles)

    place.interface(1, planes((own_b,), cy), planes((got_b,), cy), got_db, got_y, cz, cy, layers, finish)

    low_has = jnp.where(odd == 1, has[0], has[1])
    high_has = jnp.where(odd == 1, has[1], has[0])

    def either(a, b):
        return [jnp.where(odd == 1, x, y) for x, y in zip(a, b)], [jnp.where(odd == 1, y, x) for x, y in zip(a, b)]

    def along(plane, pairs):
        low = place.scale(place.flank([p[0] for p in pairs], True), low_has)
        high = place.scale(place.flank([p[1] for p in pairs], False), high_has)
        return [low] + plane + [high]

    def inner_y(k):
        pairs = [either(place.diag(got_da, k, j=j), place.diag(got_db, k, j=j)) for j in range(3 - k)]
        return along(load(got_y, k * cz, cz // SUB), pairs)

    def outer_y(k):
        pairs = [either(place.near(got_a, k * cy, cy, 0), place.near(got_b, k * cy, cy, 0))] if k < 2 else []
        if k == 0:
            pairs.append(either([jnp.broadcast_to(got_a[c, 4 * cy:4 * cy + 1, :], (SUB, LANES)) for c in range(chunks)], place.row(got_b, 4 * cy, 0)))
        return along(load(own_y, k * cz, cz // SUB), pairs)

    def mask_y(tiles):
        return [place.scale(tiles[0], low_has)] + tiles[1:-1] + [place.scale(tiles[-1], high_has)]

    flat = pot.reshape(chunks * cells, LANES)

    def finish_y(j, tiles):
        row = jnp.where(right, j, cy - 1 - j)
        for c in range(chunks):
            for half in range(cz // SUB):
                where = (pl.ds(c * cells + half * SUB * cy + row, SUB, stride=cy), slice(None))
                flat[where] = flat[where] + tiles[half + 1][c]

    respond(cz + 2 * SUB, outer_y, inner_y, mask_y, columns, finish_y)

    last = leaving(pot, reach, deep, 0, cy, 1) + leaving(pot, rest, cz - deep, edge, SUB, 2)
    for c in last:
        c.start()

    wide = picked.shape[0]

    def pick(g, carry):
        for u in range(16):
            i = g * 16 + u
            picked[pl.ds(i, 1), :] = flat[pl.ds(row_of[i], 1), :]
        return carry

    lax.fori_loop(0, wide // 16, pick, 0)
    number = lax.broadcasted_iota(jnp.int32, (LANES, LANES), 0)
    for q in range(wide // LANES):
        turned = picked[q * LANES:(q + 1) * LANES, :].T
        chosen = jnp.where(number == lane_of[q:q + 1, :], turned, 0.0)
        line = jnp.sum(chosen, axis=0, keepdims=True)
        values[:, :, q * LANES:(q + 1) * LANES] = jnp.broadcast_to(line[None], (values.shape[0], 1, LANES))
    for c in leave + last:
        c.wait()


def join(row_of, lane_of, block, own, got, devices):
    chunks, cells, _ = block.shape
    cy = (own[0].shape[1] - SUB) // 4
    cz = cells // cy
    nodes = row_of.shape[0]
    return pl.pallas_call(
        join_kernel,
        out_shape=(f32(cz, cy, chunks * LANES), f32(devices, 1, nodes)),
        in_specs=[SMEM, VMEM, VMEM] + [VMEM] * 7,
        out_specs=(ANY, VMEM),
        scratch_shapes=[
            pltpu.VMEM((chunks, cells, LANES), jnp.float32),
            pltpu.VMEM((SLOTS, chunks, cy + 2 * SUB + 2 * PAD, LANES), jnp.float32),
            pltpu.VMEM((SLOTS, chunks, cz + 2 * SUB + 2 * PAD, LANES), jnp.float32),
            pltpu.VMEM((nodes, LANES), jnp.float32),
            pltpu.SemaphoreType.DMA((3, chunks)),
        ],
        compiler_params=pltpu.CompilerParams(vmem_limit_bytes=24 << 20),
        name="join",
    )(row_of, lane_of, block, *own, *got)


def window_kernel(table_ref, slot_ref, matrix_ref, hot_ref, keep_ref, send_ref, rows_ref):
    rows, columns = matrix_ref.shape
    owners, _, width = table_ref.shape
    parts = width // LANES
    count = owners * parts
    for q in range(parts):
        rows_ref[pl.ds(q, owners, stride=parts), :] = table_ref[:, 0, q * LANES:(q + 1) * LANES]
    turned = rows_ref[...].T
    high_part = turned.astype(jnp.bfloat16)
    low_part = (turned - high_part.astype(jnp.float32)).astype(jnp.bfloat16)
    halves = jnp.concatenate([high_part, low_part], axis=0)
    number = lax.broadcasted_iota(jnp.int32, (count, LANES), 0)
    deep = lax.broadcasted_iota(jnp.int32, (LANES, LANES), 0)
    blocks = rows // 16
    chunks = columns // LANES
    each = WINDOW_CHUNKS
    col = lax.axis_index("cols").astype(jnp.int32)
    first = col * chunks
    start = [pl.multiple_of(side * (rows // 2), SUB) for side in (col, 1 - col)]

    def part(i, accs):
        accs = list(accs)
        slots = [slot_ref[pl.ds(first + i * each + u, 1), :] for u in range(each)]
        at = i * (each * LANES)
        if hot_ref.shape[0] == count:
            hot = hot_ref[:, pl.ds(at if isinstance(i, int) else pl.multiple_of(at, LANES), each * LANES)]
        else:
            hot = jnp.concatenate([one_hot(s, number) for s in slots], axis=1)
        found = jnp.dot(halves, hot, preferred_element_type=jnp.float32)
        for u in range(each):
            both = found[:LANES, u * LANES:(u + 1) * LANES] + found[LANES:, u * LANES:(u + 1) * LANES]
            lane = jnp.broadcast_to(slots[u] & (LANES - 1), (LANES, LANES))
            line = jnp.sum(jnp.where(deep == lane, both, 0.0), axis=0, keepdims=True)
            value = jnp.broadcast_to(line, (SUB, LANES))
            at = i * (each * LANES) + u * LANES
            at = at if isinstance(i, int) else pl.multiple_of(at, LANES)
            for side in range(2):
                for b in range(blocks):
                    tile = matrix_ref[pl.ds(start[side] + SUB * b, SUB), pl.ds(at, LANES)]
                    accs[side * blocks + b] = accs[side * blocks + b] + tile * value
        return tuple(accs)

    zero = jnp.zeros((SUB, LANES), jnp.float32)
    accs = (zero,) * (2 * blocks)
    if chunks // each <= 4:
        for i in range(chunks // each):
            accs = part(i, accs)
    else:
        accs = lax.fori_loop(0, chunks // each, part, accs)
    for side, out in enumerate((keep_ref, send_ref)):
        tall = jnp.concatenate(list(accs[side * blocks:(side + 1) * blocks]) + [zero] * (16 - blocks), axis=0)
        out[...] = jnp.sum(tall.T, axis=0, keepdims=True)


WINDOW_CHUNKS = 24


def window_product(table, slots, matrix, hot):
    rows, columns = matrix.shape
    assert columns % (WINDOW_CHUNKS * LANES) == 0 and rows % 16 == 0 and rows <= 2 * LANES
    out = f32(1, LANES)
    return pl.pallas_call(
        window_kernel,
        out_shape=(out, out),
        in_specs=[VMEM] * 4,
        out_specs=(VMEM, VMEM),
        scratch_shapes=[pltpu.VMEM((table.size // LANES, LANES), jnp.float32)],
        compiler_params=pltpu.CompilerParams(vmem_limit_bytes=32 << 20),
        name="window",
    )(table, slots, matrix, hot)


def routes(n):
    def across(r):
        other = r + 1 if r % 2 else r - 1
        return other if 0 <= other < n else None

    near = [(r, r ^ 1) for r in range(n)]
    far, near_diag, far_diag = [], [], []
    for r in range(n):
        for c in range(2):
            other = across(r)
            far.append((r * 2 + c, r * 2 + 1 - c if other is None else other * 2 + c))
            near_diag.append((r * 2 + c, (r ^ 1) * 2 + 1 - c))
            far_diag.append((r * 2 + c, (r if other is None else other) * 2 + 1 - c))
    return near, far, near_diag, far_diag


def local(phi_start, source, owner_voxel, column_slot, layer_matrix):
    n = lax.axis_size("rows")
    assert lax.axis_size("cols") == 2 and n % 2 == 0
    devices = 2 * n
    cz, cy, nx = phi_start.shape
    near, far, near_diag, far_diag = routes(n)
    swap = [(0, 1), (1, 0)]

    pack_b, diag_b = far_face(phi_start, source)
    got_b = lax.ppermute(pack_b, BOTH, far)
    pack_a, pack_y, diag_a = near_face(diag_b, phi_start, source)
    got_db = lax.ppermute(diag_b, BOTH, far_diag)
    got_y = lax.ppermute(pack_y, "cols", swap)
    got_da = lax.ppermute(diag_a, BOTH, near_diag)
    got_a = lax.ppermute(pack_a, "rows", near)
    slots = column_slot.reshape(-1, LANES)
    block, matrix, hot = alone(phi_start, source, layer_matrix, slots)
    x = owner_voxel % nx
    row_of = (x // LANES) * (cz * cy) + owner_voxel // nx
    lane_of = (x % LANES).reshape(-1, LANES)
    block = near_join(pack_a, got_a, got_da, got_y, block)
    potential, values = join(
        row_of, lane_of, block, (pack_b, pack_y), (got_a, got_b, got_y, got_da, got_db), devices
    )
    table = lax.all_to_all(values, BOTH, 0, 0, tiled=True)
    keep, send = window_product(table, slots, matrix, hot)
    received = lax.ppermute(send, "cols", swap)
    half = layer_matrix.shape[0] // 2
    return potential, (keep + received)[0, :half]


def solution(mesh):
    return jax.shard_map(
        local,
        mesh=mesh,
        in_specs=(
            P("rows", "cols", None),
            P("rows", "cols", None),
            P(("rows", "cols")),
            P(),
            P("rows", "cols"),
        ),
        out_specs=(P("rows", "cols", None), P(("rows", "cols"))),
        check_vma=False,
    )
```

```python
import functools

import jax
import jax.numpy as jnp
from jax import lax
from jax.experimental import pallas as pl
from jax.experimental.pallas import tpu as pltpu
from jax.sharding import PartitionSpec as P

ITERS = 4
LANES = 128
SUB = 8
SIXTH = 1.0 / 6.0
LITTLE = pl.CostEstimate(flops=1, bytes_accessed=1, transcendentals=0)
FIRST_LIMIT = 58 << 20
BOTH = ("rows", "cols")
VMEM = pl.BlockSpec(memory_space=pltpu.VMEM)
SMEM = pl.BlockSpec(memory_space=pltpu.SMEM)
ANY = pl.BlockSpec(memory_space=pl.ANY)


def lanes_of(shape=(SUB, LANES)):
    return lax.broadcasted_iota(jnp.int32, shape, 1)


def subs_of(shape=(SUB, LANES)):
    return lax.broadcasted_iota(jnp.int32, shape, 0)


PAD = SUB


def around(ref, slot, rows):
    chunks = ref.shape[1]
    lane = lanes_of()
    zero = jnp.zeros((SUB, LANES), jnp.float32)
    out = []
    for b in range(rows // SUB):
        at = PAD + SUB * b
        here = [ref[slot, c, pl.ds(at, SUB), :] for c in range(chunks)]
        before = [pltpu.roll(t, 1, 1) for t in here]
        after = [pltpu.roll(t, LANES - 1, 1) for t in here]
        row = []
        for c in range(chunks):
            west = jnp.where(lane == 0, before[c - 1] if c else zero, before[c])
            east = jnp.where(lane == LANES - 1, after[c + 1] if c + 1 < chunks else zero, after[c])
            row.append((west + east) + (ref[slot, c, pl.ds(at - 1, SUB), :] + ref[slot, c, pl.ds(at + 1, SUB), :]))
        out.append(row)
    return out


def layer_of(ref, slot, rows):
    return [[ref[slot, c, pl.ds(PAD + SUB * b, SUB), :] for c in range(ref.shape[1])] for b in range(rows // SUB)]


def keep_layer(ref, slot, tiles):
    for b, row in enumerate(tiles):
        for c, tile in enumerate(row):
            ref[slot, c, pl.ds(PAD + SUB * b, SUB), :] = tile


def clear_pads(ref, slot, rows):
    zero = jnp.zeros((SUB, LANES), jnp.float32)
    for c in range(ref.shape[1]):
        ref[slot, c, 0:PAD, :] = zero
        ref[slot, c, PAD + rows:2 * PAD + rows, :] = zero


def load(ref, at, blocks):
    return [[ref[c, pl.ds(at + SUB * b, SUB), :] for c in range(ref.shape[0])] for b in range(blocks)]


def store(ref, at, tiles):
    for b, row in enumerate(tiles):
        for c, tile in enumerate(row):
            ref[c, pl.ds(at + SUB * b, SUB), :] = tile


def total(*terms):
    terms = [t for t in terms if t is not None]
    out = []
    for b in range(len(terms[0])):
        row = []
        for c in range(len(terms[0][0])):
            value = terms[0][b][c]
            for t in terms[1:]:
                value = value + t[b][c]
            row.append(value * SIXTH)
        out.append(row)
    return out


def spread(tile, i):
    return jnp.broadcast_to(tile[i:i + 1, :], (SUB, LANES))


def stack(rows):
    sub = subs_of()
    out = []
    for c in range(len(rows[0])):
        value = rows[0][c]
        for i in range(1, len(rows)):
            value = jnp.where(sub == i, rows[i][c], value)
        out.append(value)
    return out


def near_row(right, first, last, m):
    return [jnp.where(right, spread(f, m), spread(t, SUB - 1 - m)) for f, t in zip(first, last)]


def solve_face(first, source, p0, work, put, rows):
    first(0)
    put(0, layer_of(p0, 0, rows))
    for j in range(3):
        first(j + 1)
        back = layer_of(p0, j - 1, rows) if j else None
        keep_layer(work, j, total(source(j), around(p0, j, rows), layer_of(p0, j + 1, rows), back))
    one = [layer_of(work, j, rows) for j in range(3)]
    put(1, one[0])
    for j in range(2):
        keep_layer(work, 3 + j, total(source(j), around(work, j, rows), one[j + 1], one[j - 1] if j else None))
    two = [layer_of(work, 3 + j, rows) for j in range(2)]
    put(2, two[0])
    put(3, total(source(0), around(work, 3, rows), two[1]))


def fetch_face(phi, src, low, raw, sem):
    last = phi.shape[0] - 1
    copies = {}
    for i, j in ((0, 0), (0, 1), (1, 0), (0, 2), (1, 1), (0, 3), (1, 2)):
        z = jnp.where(low == 1, j, last - j)
        copies[i, j] = pltpu.make_async_copy((src if i else phi).at[z], raw.at[i, j], sem.at[i, j])
    return copies


def tiles_of(ref):
    rows, wide = ref.shape
    return [[ref[SUB * b:SUB * b + SUB, c * LANES:(c + 1) * LANES] for c in range(wide // LANES)] for b in range(rows // SUB)]


def send_face(right, first, source, p0, work, put, diag, cy):
    chunks = p0.shape[1]
    solve_face(first, source, p0, work, put, cy)

    def near(ref, slot, m):
        edges = [[ref[slot, c, pl.ds(at, SUB), :] for c in range(chunks)] for at in (PAD, PAD + cy - SUB)]
        return near_row(right, *edges, m)

    put(4, [near(p0, 1, 0)])
    store(diag, 0, [stack([
        near(p0, 0, 0), near(p0, 1, 0), near(p0, 2, 0), near(work, 0, 0), near(work, 1, 0),
        near(work, 3, 0), near(p0, 0, 1), near(p0, 0, 2),
    ])])
    store(diag, SUB, [near(work, 0, 1)])


def far_face_kernel(phi, src, pack, diag, raw, p0, work, sem):
    cy = phi.shape[1]
    odd, col, _ = whereabouts()
    copies = fetch_face(phi, src, 1 - odd, raw, sem)
    for c in copies.values():
        c.start()
    for i in range(4):
        clear_pads(p0, i, cy)
    for i in range(5):
        clear_pads(work, i, cy)
    def first(j):
        copies[0, j].wait()
        keep_layer(p0, j, tiles_of(raw.at[0, j]))

    def source(j, seen=set()):
        if j not in seen:
            seen.add(j)
            copies[1, j].wait()
        return tiles_of(raw.at[1, j])

    send_face(col == 1, first, source, p0, work, lambda k, tiles: store(pack, k * cy, tiles), diag, cy)


def f32(*shape):
    return jax.ShapeDtypeStruct(shape, jnp.float32)


def face_scratch(chunks, cy):
    tall = cy + 2 * PAD
    return [
        pltpu.VMEM((2, 4, cy, chunks * LANES), jnp.float32),
        pltpu.VMEM((4, chunks, tall, LANES), jnp.float32),
        pltpu.VMEM((5, chunks, tall, LANES), jnp.float32),
    ]


def whereabouts():
    n, r = lax.axis_size("rows"), lax.axis_index("rows").astype(jnp.int32)
    odd = lax.rem(r, 2)
    return odd, lax.axis_index("cols").astype(jnp.int32), jnp.where(odd == 1, r < n - 1, r > 0).astype(jnp.int32)


def far_face(phi, src):
    cz, cy, nx = phi.shape
    chunks = nx // LANES
    return pl.pallas_call(
        far_face_kernel,
        out_shape=(f32(chunks, 4 * cy + SUB, LANES), f32(chunks, 2 * SUB, LANES)),
        in_specs=[ANY, ANY],
        out_specs=(VMEM, VMEM),
        scratch_shapes=face_scratch(chunks, cy) + [pltpu.SemaphoreType.DMA((2, 4))],
        compiler_params=pltpu.CompilerParams(vmem_limit_bytes=FIRST_LIMIT),
        name="far_face",
    )(phi, src)


def near_face_kernel(after, phi, src, pack, pack_y, diag, p0, work, edge, edge_p, edge_w):
    cz, cy, nx = phi.shape
    chunks = nx // LANES
    odd, col, _ = whereabouts()
    right = col == 1
    for i in range(4):
        clear_pads(p0, i, cy)
        clear_pads(edge_p, i, cz)
    for i in range(5):
        clear_pads(work, i, cy)
        clear_pads(edge_w, i, cz)

    def layer(j):
        return jnp.where(odd == 1, j, cz - 1 - j)

    def first(j):
        keep_layer(p0, j, tiles_of(phi.at[layer(j)]))

    def put(k, tiles):
        if k < 4:
            store(pack, k * cy, tiles)
        else:
            for c, tile in enumerate(tiles[0]):
                pack[c, k * cy:k * cy + 1, :] = tile[:1, :]

    send_face(right, first, lambda j: tiles_of(src.at[layer(j)]), p0, work, put, diag, cy)
    at = pl.multiple_of(jnp.where(right, 0, cy - SUB), SUB)
    for i, whole in enumerate((phi, src)):
        for z in range(cz):
            for c in range(chunks):
                edge[i, c, z * SUB:(z + 1) * SUB, :] = whole[z, pl.ds(at, SUB), c * LANES:(c + 1) * LANES]
    flat = edge.reshape(2 * chunks * cz * SUB, LANES)

    def plane(i, c, m):
        row = jnp.where(right, m, SUB - 1 - m)
        return flat[pl.ds((i * chunks + c) * cz * SUB + row, cz, stride=SUB), :]

    def first_plane(m):
        for c in range(chunks):
            edge_p[m, c, PAD:PAD + cz, :] = plane(0, c, m)

    def source(m):
        whole = [plane(1, c, m) for c in range(chunks)]
        return [[w[SUB * b:SUB * b + SUB, :] for w in whole] for b in range(cz // SUB)]

    solve_face(first_plane, source, edge_p, edge_w, lambda k, tiles: store(pack_y, k * cz, tiles), cz)
    ends = [[edge_p[1, c, pl.ds(PAD + i, 1), :] for c in range(chunks)] for i in (0, cz - 1)]
    ends = [[jnp.broadcast_to(t, (SUB, LANES)) for t in row] for row in ends]
    own = [[jnp.where(odd == 1, a, b) for a, b in zip(*ends)], [jnp.where(odd == 1, b, a) for a, b in zip(*ends)]]
    store(pack_y, 4 * cz, [stack(own)])


def near_face(after, phi, src):
    cz, cy, nx = phi.shape
    chunks = nx // LANES
    tall = cz + 2 * PAD
    return pl.pallas_call(
        near_face_kernel,
        out_shape=(
            f32(chunks, 4 * cy + 1, LANES), f32(chunks, 4 * cz + SUB, LANES), f32(chunks, 2 * SUB, LANES),
        ),
        in_specs=[ANY, VMEM, VMEM],
        out_specs=(VMEM,) * 3,
        scratch_shapes=face_scratch(chunks, cy)[1:] + [
            pltpu.VMEM((2, chunks, cz * SUB, LANES), jnp.float32),
            pltpu.VMEM((4, chunks, tall, LANES), jnp.float32),
            pltpu.VMEM((5, chunks, tall, LANES), jnp.float32),
        ],
        compiler_params=pltpu.CompilerParams(vmem_limit_bytes=24 << 20),
        cost_estimate=LITTLE,
        name="near_face",
    )(after, phi, src)


def alone_kernel(phi, src, matrix, slots, out, matrix_out, hot, buf_a, buf_b, sem):
    cz, cy, nx = phi.shape
    blocks, chunks = cy // SUB, nx // LANES
    pieces = 4
    deep = matrix.shape[0] // pieces
    copies = [
        pltpu.make_async_copy(matrix.at[i * deep:(i + 1) * deep], matrix_out.at[i * deep:(i + 1) * deep], sem.at[i])
        for i in range(pieces)
    ]
    for c in copies:
        c.start()
    zero = [[jnp.zeros((SUB, LANES), jnp.float32)] * chunks] * blocks
    for ref in (buf_a, buf_b):
        for z in (0, cz + 1):
            keep_layer(ref, z, zero)

    def begin(z, carry):
        for ref in (buf_a, buf_b):
            clear_pads(ref, z + 1, cy)
        keep_layer(buf_a, z + 1, tiles_of(phi.at[z]))
        return carry

    lax.fori_loop(0, cz, begin, 0)
    for k in range(ITERS):
        here, there = (buf_a, buf_b) if k % 2 == 0 else (buf_b, buf_a)

        def layer(z, carry, here=here, there=there, last=k == ITERS - 1):
            value = total(tiles_of(src.at[z]), around(here, z + 1, cy), layer_of(here, z, cy), layer_of(here, z + 2, cy))
            if last:
                for c in range(chunks):
                    for b in range(blocks):
                        out[c, pl.ds(pl.multiple_of(z * cy, SUB) + SUB * b, SUB), :] = value[b][c]
            else:
                keep_layer(there, z + 1, value)
            return carry

        lax.fori_loop(0, cz, layer, 0, unroll=True)
    if hot.shape[0] == slots.shape[0]:
        first = lax.axis_index("cols").astype(jnp.int32) * (hot.shape[1] // LANES)
        number = lax.broadcasted_iota(jnp.int32, (hot.shape[0], LANES), 0)
        for u in range(hot.shape[1] // LANES):
            hot[:, u * LANES:(u + 1) * LANES] = one_hot(slots[pl.ds(first + u, 1), :], number)
    for c in copies:
        c.wait()


def alone(phi, src, matrix, slots):
    cz, cy, nx = phi.shape
    chunks = nx // LANES
    count, columns = slots.shape[0], matrix.shape[1]
    ahead = (count, columns) if count * columns <= 4 << 20 else (2 * SUB, LANES)
    return pl.pallas_call(
        alone_kernel,
        out_shape=(f32(chunks, cz * cy, LANES), f32(*matrix.shape), jax.ShapeDtypeStruct(ahead, jnp.bfloat16)),
        in_specs=[VMEM, VMEM, ANY, VMEM],
        out_specs=(VMEM,) * 3,
        scratch_shapes=[
            pltpu.VMEM((cz + 2, chunks, cy + 2 * PAD, LANES), jnp.float32),
            pltpu.VMEM((cz + 2, chunks, cy + 2 * PAD, LANES), jnp.float32),
            pltpu.SemaphoreType.DMA((4,)),
        ],
        compiler_params=pltpu.CompilerParams(vmem_limit_bytes=20 << 20),
        cost_estimate=LITTLE,
        name="alone",
    )(phi, src, matrix, slots)


def respond(rows, outer, inner, mask, work, finish):
    for slot in range(SLOTS):
        clear_pads(work, slot, rows)
    o0, i0, o0_2, i0_2, o1_2, i1_2, o0_3, i0_3, i1_3, i2_3 = range(SLOTS)

    def keep(slot, *terms):
        keep_layer(work, slot, mask(total(*terms)))

    def at(slot):
        return layer_of(work, slot, rows)

    def near(slot):
        return around(work, slot, rows)

    keep(o0, outer(0))
    keep(i0, inner(0))
    keep(o0_2, outer(1), near(o0), at(i0))
    keep(i0_2, inner(1), near(i0), at(o0))
    keep(o1_2, at(o0))
    keep(i1_2, at(i0))
    keep(o0_3, outer(2), near(o0_2), at(o1_2), at(i0_2))
    keep(i0_3, inner(2), near(i0_2), at(o0_2), at(i1_2))
    keep(i1_3, near(i1_2), at(i0_2))
    keep(i2_3, at(i1_2))
    finish(0, total(inner(3), near(i0_3), at(o0_3), at(i1_3)))
    finish(1, total(near(i1_3), at(i0_3), at(i2_3)))
    finish(2, total(near(i2_3), at(i1_3)))
    finish(3, total(at(i2_3)))


SLOTS = 10


def planes(refs, cy):
    each = 4 // len(refs)
    return lambda k: load(refs[k // each], k % each * cy, cy // SUB)


class Corner:
    def __init__(self, chunks):
        self.odd, col, has_far = whereabouts()
        self.right = col == 1
        self.has = (1.0, has_far.astype(jnp.float32))
        self.zero = [jnp.zeros((SUB, LANES), jnp.float32)] * chunks
        self.at_low = jnp.where(self.right, 1.0, 0.0)
        self.at_high = 1.0 - self.at_low

    def row(self, ref, at, i):
        return [spread(t, i) for t in load(ref, at, 1)[0]]

    def scale(self, tiles, factor):
        return [t * factor for t in tiles]

    def flank(self, rows, low):
        out, sub = self.zero, subs_of()
        for m, value in enumerate(rows):
            out = [jnp.where(sub == (SUB - 1 - m if low else m), v, o) for v, o in zip(value, out)]
        return out

    def near(self, ref, at, cy, m):
        return near_row(self.right, load(ref, at, 1)[0], load(ref, at + cy - SUB, 1)[0], m)

    def diag(self, ref, k, j=0, m=0):
        place = {(0, 0, 0): 0, (0, 1, 0): 1, (0, 2, 0): 2, (1, 0, 0): 3, (1, 1, 0): 4, (2, 0, 0): 5, (0, 0, 1): 6,
                 (0, 0, 2): 7, (1, 0, 1): 8}[(k, j, m)]
        return self.row(ref, place // SUB * SUB, place % SUB)

    def low_side(self, i):
        return self.odd if i == 0 else 1 - self.odd

    def add_layer(self, pot, i, j, cz, cy, tiles):
        start = pl.multiple_of(jnp.where(self.low_side(i) == 1, j, cz - 1 - j) * cy, SUB)
        for b, row in enumerate(tiles):
            for c, tile in enumerate(row):
                where = (c, pl.ds(start + SUB * b, SUB), slice(None))
                pot[where] = pot[where] + tile

    def interface(self, i, own, got, got_d, got_y, cz, cy, work, finish):
        low, blocks = self.low_side(i) == 1, cy // SUB

        def end_row(k):
            return [jnp.where(low, a, b) for a, b in zip(self.row(got_y, k * cz, 0), self.row(got_y, k * cz + cz - SUB, SUB - 1))]

        def driven(plane, rows):
            middle = [self.scale(t, self.has[i]) for t in plane]
            return ([self.scale(self.flank(rows, True), self.has[i] * self.at_low)] + middle
                    + [self.scale(self.flank(rows, False), self.has[i] * self.at_high)])

        def inner(k):
            return driven(got(k), [self.diag(got_d, k, m=m) for m in range(3 - k)])

        def outer(k):
            rows = [end_row(k)] if k < 2 else []
            if k == 0:
                rows.append(self.row(got_y, 4 * cz, i))
            return driven(own(k), rows)

        def mask(tiles):
            return [self.scale(tiles[0], self.at_low)] + tiles[1:-1] + [self.scale(tiles[-1], self.at_high)]

        respond(cy + 2 * SUB, outer, inner, mask, work, lambda j, tiles: finish(j, tiles[1:-1]))


def near_join_kernel(own, got, got_d, got_y, block, out, work):
    chunks, cells, _ = block.shape
    cy = (own.shape[1] - 1) // 4
    cz = cells // cy
    place = Corner(chunks)
    for z in range(cz):
        store(out, z * cy, load(block, z * cy, cy // SUB))
    place.interface(
        0, planes((own,), cy), planes((got,), cy), got_d, got_y, cz, cy, work,
        lambda j, tiles: place.add_layer(out, 0, j, cz, cy, tiles),
    )


def one_hot(slots, number):
    return jnp.where(number == jnp.broadcast_to(slots >> 7, number.shape), 1.0, 0.0).astype(jnp.bfloat16)


def near_join(own, got, got_d, got_y, block):
    chunks, tall, _ = own.shape
    cy = (tall - 1) // 4
    return pl.pallas_call(
        near_join_kernel,
        out_shape=f32(*block.shape),
        in_specs=[VMEM] * 5,
        out_specs=VMEM,
        scratch_shapes=[pltpu.VMEM((SLOTS, chunks, cy + 2 * SUB + 2 * PAD, LANES), jnp.float32)],
        compiler_params=pltpu.CompilerParams(vmem_limit_bytes=24 << 20),
        name="near_join",
    )(own, got, got_d, got_y, block)


def join_kernel(
    row_of, lane_of, block, own_b, own_y, got_a, got_b, got_y, got_da, got_db,
    potential, values, pot, layers, columns, picked, sem,
):
    chunks, cells, _ = pot.shape
    cy = (own_b.shape[1] - SUB) // 4
    cz = cells // cy
    blocks = cy // SUB
    place = Corner(chunks)
    odd, right, has = place.odd, place.right, place.has
    deep = 4
    low_b = place.low_side(1) == 1
    rest, reach = jnp.where(low_b, deep, 0), jnp.where(low_b, 0, cz - deep)
    edge = pl.multiple_of(jnp.where(right, 0, cy - SUB), SUB)
    inner_rows = pl.multiple_of(jnp.where(right, SUB, 0), SUB)

    def leaving(ref, z, layers_out, y, rows, i):
        whole = ref.reshape(chunks, cz, cy, LANES)
        return [
            pltpu.make_async_copy(
                whole.at[c, pl.ds(z, layers_out), pl.ds(y, rows), :],
                potential.at[pl.ds(z, layers_out), pl.ds(y, rows), pl.ds(c * LANES, LANES)],
                sem.at[i, c],
            )
            for c in range(chunks)
        ]

    leave = leaving(block, rest, cz - deep, inner_rows, cy - SUB, 0)
    for c in leave:
        c.start()
    for i in range(cz - deep):
        start = pl.multiple_of((rest + i) * cy, SUB)
        store(pot, start, load(block, start, blocks))

    def finish(j, tiles):
        start = pl.multiple_of(jnp.where(low_b, j, cz - 1 - j) * cy, SUB)
        before = load(block, start, blocks)
        store(pot, start, [[b + t for b, t in zip(*rows)] for rows in zip(before, tiles)])

    place.interface(1, planes((own_b,), cy), planes((got_b,), cy), got_db, got_y, cz, cy, layers, finish)

    low_has = jnp.where(odd == 1, has[0], has[1])
    high_has = jnp.where(odd == 1, has[1], has[0])

    def either(a, b):
        return [jnp.where(odd == 1, x, y) for x, y in zip(a, b)], [jnp.where(odd == 1, y, x) for x, y in zip(a, b)]

    def along(plane, pairs):
        low = place.scale(place.flank([p[0] for p in pairs], True), low_has)
        high = place.scale(place.flank([p[1] for p in pairs], False), high_has)
        return [low] + plane + [high]

    def inner_y(k):
        pairs = [either(place.diag(got_da, k, j=j), place.diag(got_db, k, j=j)) for j in range(3 - k)]
        return along(load(got_y, k * cz, cz // SUB), pairs)

    def outer_y(k):
        pairs = [either(place.near(got_a, k * cy, cy, 0), place.near(got_b, k * cy, cy, 0))] if k < 2 else []
        if k == 0:
            pairs.append(either([jnp.broadcast_to(got_a[c, 4 * cy:4 * cy + 1, :], (SUB, LANES)) for c in range(chunks)], place.row(got_b, 4 * cy, 0)))
        return along(load(own_y, k * cz, cz // SUB), pairs)

    def mask_y(tiles):
        return [place.scale(tiles[0], low_has)] + tiles[1:-1] + [place.scale(tiles[-1], high_has)]

    flat = pot.reshape(chunks * cells, LANES)

    def finish_y(j, tiles):
        row = jnp.where(right, j, cy - 1 - j)
        for c in range(chunks):
            for half in range(cz // SUB):
                where = (pl.ds(c * cells + half * SUB * cy + row, SUB, stride=cy), slice(None))
                flat[where] = flat[where] + tiles[half + 1][c]

    respond(cz + 2 * SUB, outer_y, inner_y, mask_y, columns, finish_y)

    last = leaving(pot, reach, deep, 0, cy, 1) + leaving(pot, rest, cz - deep, edge, SUB, 2)
    for c in last:
        c.start()

    wide = picked.shape[0]

    def pick(g, carry):
        for u in range(16):
            i = g * 16 + u
            picked[pl.ds(i, 1), :] = flat[pl.ds(row_of[i], 1), :]
        return carry

    lax.fori_loop(0, wide // 16, pick, 0)
    number = lax.broadcasted_iota(jnp.int32, (LANES, LANES), 0)
    for q in range(wide // LANES):
        turned = picked[q * LANES:(q + 1) * LANES, :].T
        chosen = jnp.where(number == lane_of[q:q + 1, :], turned, 0.0)
        line = jnp.sum(chosen, axis=0, keepdims=True)
        values[:, :, q * LANES:(q + 1) * LANES] = jnp.broadcast_to(line[None], (values.shape[0], 1, LANES))
    for c in leave + last:
        c.wait()


def join(row_of, lane_of, block, own, got, devices):
    chunks, cells, _ = block.shape
    cy = (own[0].shape[1] - SUB) // 4
    cz = cells // cy
    nodes = row_of.shape[0]
    return pl.pallas_call(
        join_kernel,
        out_shape=(f32(cz, cy, chunks * LANES), f32(devices, 1, nodes)),
        in_specs=[SMEM, VMEM, VMEM] + [VMEM] * 7,
        out_specs=(ANY, VMEM),
        scratch_shapes=[
            pltpu.VMEM((chunks, cells, LANES), jnp.float32),
            pltpu.VMEM((SLOTS, chunks, cy + 2 * SUB + 2 * PAD, LANES), jnp.float32),
            pltpu.VMEM((SLOTS, chunks, cz + 2 * SUB + 2 * PAD, LANES), jnp.float32),
            pltpu.VMEM((nodes, LANES), jnp.float32),
            pltpu.SemaphoreType.DMA((3, chunks)),
        ],
        compiler_params=pltpu.CompilerParams(vmem_limit_bytes=24 << 20),
        name="join",
    )(row_of, lane_of, block, *own, *got)


def window_kernel(table_ref, slot_ref, matrix_ref, hot_ref, keep_ref, send_ref, rows_ref):
    rows, columns = matrix_ref.shape
    owners, _, width = table_ref.shape
    parts = width // LANES
    count = owners * parts
    for q in range(parts):
        rows_ref[pl.ds(q, owners, stride=parts), :] = table_ref[:, 0, q * LANES:(q + 1) * LANES]
    turned = rows_ref[...].T
    high_part = turned.astype(jnp.bfloat16)
    low_part = (turned - high_part.astype(jnp.float32)).astype(jnp.bfloat16)
    halves = jnp.concatenate([high_part, low_part], axis=0)
    number = lax.broadcasted_iota(jnp.int32, (count, LANES), 0)
    deep = lax.broadcasted_iota(jnp.int32, (LANES, LANES), 0)
    blocks = rows // 16
    chunks = columns // LANES
    each = WINDOW_CHUNKS
    col = lax.axis_index("cols").astype(jnp.int32)
    first = col * chunks
    start = [pl.multiple_of(side * (rows // 2), SUB) for side in (col, 1 - col)]

    def part(i, accs):
        accs = list(accs)
        slots = [slot_ref[pl.ds(first + i * each + u, 1), :] for u in range(each)]
        at = i * (each * LANES)
        if hot_ref.shape[0] == count:
            hot = hot_ref[:, pl.ds(at if isinstance(i, int) else pl.multiple_of(at, LANES), each * LANES)]
        else:
            hot = jnp.concatenate([one_hot(s, number) for s in slots], axis=1)
        found = jnp.dot(halves, hot, preferred_element_type=jnp.float32)
        for u in range(each):
            both = found[:LANES, u * LANES:(u + 1) * LANES] + found[LANES:, u * LANES:(u + 1) * LANES]
            lane = jnp.broadcast_to(slots[u] & (LANES - 1), (LANES, LANES))
            line = jnp.sum(jnp.where(deep == lane, both, 0.0), axis=0, keepdims=True)
            value = jnp.broadcast_to(line, (SUB, LANES))
            at = i * (each * LANES) + u * LANES
            at = at if isinstance(i, int) else pl.multiple_of(at, LANES)
            for side in range(2):
                for b in range(blocks):
                    tile = matrix_ref[pl.ds(start[side] + SUB * b, SUB), pl.ds(at, LANES)]
                    accs[side * blocks + b] = accs[side * blocks + b] + tile * value
        return tuple(accs)

    zero = jnp.zeros((SUB, LANES), jnp.float32)
    accs = (zero,) * (2 * blocks)
    if chunks // each <= 4:
        for i in range(chunks // each):
            accs = part(i, accs)
    else:
        accs = lax.fori_loop(0, chunks // each, part, accs)
    for side, out in enumerate((keep_ref, send_ref)):
        tall = jnp.concatenate(list(accs[side * blocks:(side + 1) * blocks]) + [zero] * (16 - blocks), axis=0)
        out[...] = jnp.sum(tall.T, axis=0, keepdims=True)


WINDOW_CHUNKS = 48


def window_product(table, slots, matrix, hot):
    rows, columns = matrix.shape
    assert columns % (WINDOW_CHUNKS * LANES) == 0 and rows % 16 == 0 and rows <= 2 * LANES
    out = f32(1, LANES)
    return pl.pallas_call(
        window_kernel,
        out_shape=(out, out),
        in_specs=[VMEM] * 4,
        out_specs=(VMEM, VMEM),
        scratch_shapes=[pltpu.VMEM((table.size // LANES, LANES), jnp.float32)],
        compiler_params=pltpu.CompilerParams(vmem_limit_bytes=32 << 20),
        name="window",
    )(table, slots, matrix, hot)


def routes(n):
    def across(r):
        other = r + 1 if r % 2 else r - 1
        return other if 0 <= other < n else None

    near = [(r, r ^ 1) for r in range(n)]
    far, near_diag, far_diag = [], [], []
    for r in range(n):
        for c in range(2):
            other = across(r)
            far.append((r * 2 + c, r * 2 + 1 - c if other is None else other * 2 + c))
            near_diag.append((r * 2 + c, (r ^ 1) * 2 + 1 - c))
            far_diag.append((r * 2 + c, (r if other is None else other) * 2 + 1 - c))
    return near, far, near_diag, far_diag


def local(phi_start, source, owner_voxel, column_slot, layer_matrix):
    n = lax.axis_size("rows")
    assert lax.axis_size("cols") == 2 and n % 2 == 0
    devices = 2 * n
    cz, cy, nx = phi_start.shape
    near, far, near_diag, far_diag = routes(n)
    swap = [(0, 1), (1, 0)]

    pack_b, diag_b = far_face(phi_start, source)
    got_b = lax.ppermute(pack_b, BOTH, far)
    pack_a, pack_y, diag_a = near_face(diag_b, phi_start, source)
    got_db = lax.ppermute(diag_b, BOTH, far_diag)
    got_y = lax.ppermute(pack_y, "cols", swap)
    got_da = lax.ppermute(diag_a, BOTH, near_diag)
    got_a = lax.ppermute(pack_a, "rows", near)
    slots = column_slot.reshape(-1, LANES)
    block, matrix, hot = alone(phi_start, source, layer_matrix, slots)
    x = owner_voxel % nx
    row_of = (x // LANES) * (cz * cy) + owner_voxel // nx
    lane_of = (x % LANES).reshape(-1, LANES)
    block = near_join(pack_a, got_a, got_da, got_y, block)
    potential, values = join(
        row_of, lane_of, block, (pack_b, pack_y), (got_a, got_b, got_y, got_da, got_db), devices
    )
    table = lax.all_to_all(values, BOTH, 0, 0, tiled=True)
    keep, send = window_product(table, slots, matrix, hot)
    received = lax.ppermute(send, "cols", swap)
    half = layer_matrix.shape[0] // 2
    return potential, (keep + received)[0, :half]


def solution(mesh):
    return jax.shard_map(
        local,
        mesh=mesh,
        in_specs=(
            P("rows", "cols", None),
            P("rows", "cols", None),
            P(("rows", "cols")),
            P(),
            P("rows", "cols"),
        ),
        out_specs=(P("rows", "cols", None), P(("rows", "cols"))),
        check_vma=False,
    )
```
